32 devices in a mesh: groups: 2 (over y), sec: 4 (over z), tp: 2 (over x), pp: 2 (over core).
Axes of the slice: x: 2, y: 2, z: 4, core: 2. Of those that a mesh axis runs over, the one named last changes fastest.
Arguments:
- query: bfloat16 [512, 4096], P(('groups', 'sec'), ('tp', 'pp')), parts along dimension 0, may hold values from -8 to 8
- keys: bfloat16 [512, 1024], P(('groups', 'sec'), 'tp'), parts along dimension 0, may hold values from -4 to 4
- values: bfloat16 [512, 1024], P(('groups', 'sec'), 'tp'), parts along dimension 0, may hold values from -6 to 6
- residual: bfloat16 [512, 2048], P(('groups', 'sec')), parts along dimension 0, may hold values from -6 to 6
- out_weight: bfloat16 [4096, 2048], P(('tp', 'pp')), may hold values from -0.09375 to 0.09375
- norm_gain: float32 [2048], replicated, may hold values from 0.1 to 1.9
- expert_ids: int32 [512, 2], P(('groups', 'sec')), parts along dimension 0, may hold values from 0 to 7, all different within a row; in each aligned block of 64 rows (0 to 63, 64 to 127, ...) at most 32 rows name the same one
- gate_codes: int32 [512, 2], P(('groups', 'sec')), parts along dimension 0, may hold values from 1 to 255
- doc_lengths: int32 [16], P('groups'), parts along dimension 0, may hold values from 1 to 128, 256 in all
- w_gate: bfloat16 [4, 2048, 16384], P(('tp', 'pp'), None, 'sec'), may hold values from -0.125 to 0.125
- w_up: bfloat16 [4, 2048, 16384], P(('tp', 'pp'), None, 'sec'), may hold values from -0.125 to 0.125
- w_down: bfloat16 [4, 16384, 2048], P(('tp', 'pp'), 'sec'), may hold values from -0.0625 to 0.0625
Outputs:
- scored: bfloat16 [512, 2048], P(('groups', 'sec', 'tp', 'pp')), parts along dimension 0
The draws below stay inside these ranges and needn't reach their ends.
There are 2 independent parts, one for each index of `groups`. The reference program is written for one: setup_inputs(seed, part) draws one part's arguments, and reference() takes and returns one part's arrays. A program takes and returns all parts, laid end to end along the dimension named above; an argument that names none is the same for every part. Nothing has to cross between parts.
Inputs may be any that keep to these rules, and one draw needn't show every extreme that they name: `expert_ids`: each row names two different experts; in each aligned block of 64 rows no expert is named by more than 32 rows, and some block reaches 32. `doc_lengths`: the lengths sum to 256; the longest is exactly 128.
All inputs are finite; a program needn't handle non-finite values.
Results may differ from the reference program's by a relative error of at most 0.015.
Values may be sent and summed in bfloat16 or wider, within the bound.
A program may use at most 128 MiB of HBM per device.

```python
import math
import jax
import jax.numpy as jnp
import numpy as np
from jax import lax

D = 2048
FF = 8192
QUERY_HEAD_COUNT = 32
KEY_VALUE_HEADS = 8
HEAD_DIMENSION = 128
E = 8
DOCS = 8
BLK = 64
MOSTB = 32
SEQUENCE_TOKENS = 256
TPP = 4


def shared_keys(key):
    normal_portion = jnp.clip(jax.random.normal(jax.random.fold_in(key, 11), (SEQUENCE_TOKENS, KEY_VALUE_HEADS * HEAD_DIMENSION), jnp.float32), -4.0, 4.0)
    return normal_portion


def draw_keys(key, part):
    normal_portion = shared_keys(key)
    return normal_portion.astype(jnp.bfloat16)


def draw_query(key, part):
    drawn = jnp.clip(jax.random.normal(jax.random.fold_in(key, 12), (SEQUENCE_TOKENS, QUERY_HEAD_COUNT * HEAD_DIMENSION), jnp.float32), -4.0, 4.0)
    return drawn.astype(jnp.bfloat16)


def set_ends(result, rng, low, high):
    longest = result.shape.index(max(result.shape))
    spots = []
    for shift in (0, 1):
        where = [jax.random.randint(jax.random.fold_in(rng, axis), (), 0, length) for axis, length in enumerate(result.shape)]
        where[longest] = (where[longest] + shift) % result.shape[longest]
        spots.append(tuple(where))
    return result.at[spots[0]].set(low).at[spots[1]].set(high)


def block_levels(stream_key, dims, cuts, least, largest):
    loudness = 1.0
    for dim, blocks in cuts:
        draws = jax.random.uniform(jax.random.fold_in(jax.random.fold_in(stream_key, 6), dim), (blocks,), jnp.float32, least / len(cuts), largest / len(cuts))
        loudness = loudness * jnp.repeat(jnp.exp(draws), dims[dim] // blocks).reshape((-1,) + (1,) * (len(dims) - 1 - dim))
    return loudness


def profile(number_of, total, bound, slope):
    weights = [(1 << 20) // math.isqrt(standing ** slope) + 1 for standing in range(2, number_of + 1)]
    surplus, counts = total - bound - (number_of - 1), [1] * (number_of - 1)
    while surplus > 0:
        movable = [i for i in range(number_of - 1) if counts[i] < bound]
        mass, left = sum([weights[i] for i in movable]), surplus
        for i in movable:
            extra = min(bound - counts[i], max(1, left * weights[i] // mass), surplus)
            counts[i] = counts[i] + extra
            surplus = surplus - extra
    return np.array([bound] + counts)


def uneven(stream_key, amount, total, most, slope):
    if amount == 2:
        one = jax.random.randint(stream_key, (), max(1, total - most), min(most, total - 1) + 1)
        return jnp.stack([one, total - one])
    lengths = jnp.asarray(profile(amount, total, most, slope), jnp.int32)
    twos = (amount - 1) // 2
    source_of, sink = lengths[1:1 + 2 * twos:2], lengths[2:2 + 2 * twos:2]
    slack = jnp.minimum(source_of - 1, most - sink)
    passed = jax.random.randint(jax.random.fold_in(stream_key, 1), (twos,), 0, 1 << 20) % (slack + 1)
    lengths = lengths.at[1:1 + 2 * twos:2].set(source_of - passed).at[2:2 + 2 * twos:2].set(sink + passed)
    return lengths[jax.random.permutation(jax.random.fold_in(stream_key, 2), amount)]


def shared_out(own_key, own, number, rows, count, top, reach, slope):
    sequence = jax.random.permutation(own_key, count)
    heavy_load, ordinary = shares(count, rows * top, reach, slope, True), shares(count, rows * top, reach, slope, False)
    places = jnp.arange(count)

    def named(tallies, turn):
        used = int((tallies > 0).sum())
        fixed = max(1, used // 4)
        moved = fixed + (places - fixed + turn * (used - fixed)) % max(1, count - fixed)
        return jnp.zeros((count,), jnp.int32).at[sequence[jnp.where(places < fixed, places, moved)]].set(jnp.asarray(tallies, jnp.int32))

    tallies = jnp.where(number % 4 == 0, named(heavy_load, number // 4), named(ordinary, number - number // 4 - 1))
    mixed = jax.random.permutation(jax.random.fold_in(own, 3), count)
    source_of, taker = mixed[0:count // 2 * 2:2], mixed[1:count // 2 * 2:2]
    slack = jnp.minimum(tallies[source_of] - 1, reach - tallies[taker]) // 2
    slack = jnp.where((source_of == sequence[0]) | (taker == sequence[0]) | (tallies[taker] == 0), 0, jnp.maximum(slack, 0))
    moved = jax.random.randint(jax.random.fold_in(own, 4), (count // 2,), 0, 1 << 20) % (slack + 1)
    tallies = tallies.at[source_of].add(-moved).at[taker].add(moved)
    members = jnp.searchsorted(jnp.cumsum(tallies), jnp.arange(rows * top), side="right").astype(jnp.int32)
    listing = members.reshape(top, rows).T
    listing = listing[jax.random.permutation(jax.random.fold_in(own, 1), rows)]
    turn = jax.random.randint(jax.random.fold_in(own, 2), (rows, 1), 0, top)
    return jnp.take_along_axis(listing, (jnp.arange(top)[None, :] + turn) % top, axis=1)


def shares(number_of, total, reach, skew, full):
    weights = [(1 << 20) // math.isqrt(grade ** skew) + 1 for grade in range(1, number_of + 1)]
    largest = reach if full else min(reach, max(-(-total // number_of), total * weights[0] // sum(weights)))
    least = 1 if total - largest >= number_of - 1 else 0
    holding, spare = [largest] + [least] * (number_of - 1), total - largest - least * (number_of - 1)
    while spare > 0:
        movable = [i for i in range(1, number_of) if holding[i] < largest] or [i for i in range(1, number_of) if holding[i] < reach]
        pool, remaining = sum([weights[i] for i in movable]), spare
        for i in movable:
            addition = min(reach - holding[i], max(1, remaining * weights[i] // pool), spare)
            holding[i] = holding[i] + addition
            spare = spare - addition
    return np.array(holding)


def noise(rng, shape, width, bound, shards=(), held_as=jnp.bfloat16):
    loudness = block_levels(rng, shape, shards, -0.22, 0.18) if shards else 1.0
    array = jax.random.normal(rng, shape, jnp.float32) * width * loudness
    return jnp.minimum(jnp.maximum(array, -bound), bound).astype(held_as)


def setup_inputs(seed: int = 0, part: int = 0) -> dict:
    splits = jax.random.split(jax.random.key(seed), 13)
    part_splits = jax.random.split(jax.random.fold_in(splits[12], part), 13)
    query = draw_query(jax.random.fold_in(jax.random.fold_in(splits[12], part), 71), part)
    keys = draw_keys(jax.random.fold_in(jax.random.fold_in(splits[12], part), 71), part)
    values = noise(part_splits[2], (SEQUENCE_TOKENS, KEY_VALUE_HEADS * HEAD_DIMENSION), 1.0, 6.0, ((0, 4), (1, 2)))
    residual = noise(part_splits[3], (SEQUENCE_TOKENS, D), 1.0, 6.0, ((0, 4),))
    out_weight = noise(splits[4], (QUERY_HEAD_COUNT * HEAD_DIMENSION, D), (QUERY_HEAD_COUNT * HEAD_DIMENSION) ** -0.5, 0.09375, ((0, 4),))
    norm_gain = jnp.clip(1.0 + 0.18 * jax.random.normal(splits[5], (D,), jnp.float32), 0.1, 1.9)
    expert_ids_keys = jax.random.split(jax.random.fold_in(part_splits[6], 1), SEQUENCE_TOKENS // BLK)
    expert_ids_turns = jax.random.permutation(jax.random.fold_in(part_splits[6], 3), SEQUENCE_TOKENS // BLK)
    expert_ids = jax.vmap(lambda own, number: shared_out(jax.random.fold_in(part_splits[6], 2), own, number, BLK, E, 2, MOSTB, 2))(expert_ids_keys, expert_ids_turns).reshape((SEQUENCE_TOKENS, 2))
    gate_codes = set_ends(jax.random.randint(part_splits[7], (SEQUENCE_TOKENS, 2), 1, 256), jax.random.fold_in(part_splits[7], 1), 1, 255).astype(jnp.int32)
    doc_lengths = uneven(part_splits[8], DOCS, SEQUENCE_TOKENS, SEQUENCE_TOKENS // 2, 2).astype(jnp.int32)
    w_gate = noise(splits[9], (TPP, D, E * FF // TPP), D ** -0.5, 0.125, ((0, 4), (2, 4)))
    w_up = noise(splits[10], (TPP, D, E * FF // TPP), D ** -0.5, 0.125, ((0, 4), (2, 4)))
    w_down = noise(splits[11], (TPP, E * FF // TPP, D), FF ** -0.5, 0.0625, ((0, 4), (1, 4)))
    return dict(query=query, keys=keys, values=values, residual=residual, out_weight=out_weight, norm_gain=norm_gain, expert_ids=expert_ids, gate_codes=gate_codes, doc_lengths=doc_lengths, w_gate=w_gate, w_up=w_up, w_down=w_down)


def doc_index(positions, doc_lengths):
    doc_ends = jnp.cumsum(doc_lengths).astype(jnp.int32)
    return lax.optimization_barrier(jnp.sum((positions[:, None] >= doc_ends[None, :]).astype(jnp.int32), axis=1))

def reference(query, keys, values, residual, out_weight, norm_gain, expert_ids, gate_codes, doc_lengths, w_gate, w_up, w_down):
    positions = jnp.arange(SEQUENCE_TOKENS, dtype=jnp.int32)
    doc = doc_index(positions, doc_lengths)
    allowed = (positions[None, :] <= positions[:, None]) & (doc[None, :] == doc[:, None])
    group_width = QUERY_HEAD_COUNT // KEY_VALUE_HEADS
    scale = HEAD_DIMENSION ** (-0.5)

    def one_head(head):
        head = head.astype(jnp.int32)
        kv_head = (head // group_width).astype(jnp.int32)
        query_head = lax.dynamic_slice_in_dim(query, head * HEAD_DIMENSION, HEAD_DIMENSION, 1)
        key_head = lax.dynamic_slice_in_dim(keys, kv_head * HEAD_DIMENSION, HEAD_DIMENSION, 1)
        value_head = lax.dynamic_slice_in_dim(values, kv_head * HEAD_DIMENSION, HEAD_DIMENSION, 1)
        scores = jnp.dot(query_head, key_head.T, preferred_element_type=jnp.float32) * scale
        scores = jnp.where(allowed, scores, -1e+30)
        row_max = lax.optimization_barrier(jnp.max(scores, axis=1, keepdims=True))
        weights = jnp.where(allowed, jnp.exp(scores - row_max), 0.0)
        totals = lax.optimization_barrier(jnp.sum(weights, axis=1, keepdims=True))
        summed = jnp.dot(weights.astype(jnp.bfloat16), value_head, preferred_element_type=jnp.float32)
        return (summed / totals).astype(jnp.bfloat16)
    heads_out = lax.map(one_head, jnp.arange(QUERY_HEAD_COUNT, dtype=jnp.int32))
    attended = heads_out.transpose(1, 0, 2).reshape(SEQUENCE_TOKENS, QUERY_HEAD_COUNT * HEAD_DIMENSION)
    stream = residual.astype(jnp.float32) + jnp.dot(attended, out_weight, preferred_element_type=jnp.float32)
    meansq = lax.optimization_barrier(jnp.mean(stream * stream, axis=1, keepdims=True))
    normed = (stream * lax.rsqrt(meansq + 1e-05) * norm_gain).astype(jnp.bfloat16)
    codes = gate_codes.astype(jnp.float32)
    share = codes / lax.optimization_barrier(jnp.sum(codes, axis=1, keepdims=True))
    block_width = FF // TPP
    capacity = SEQUENCE_TOKENS // BLK * MOSTB

    def add_expert(expert, total):
        expert = jnp.asarray(expert).astype(jnp.int32)
        hits = expert_ids == expert
        member = lax.optimization_barrier(jnp.sum(hits.astype(jnp.int32), axis=1))
        coef = lax.optimization_barrier(jnp.sum(jnp.where(hits, share, 0.0), axis=1))
        order = jnp.argsort(1 - member, stable=True)[:capacity].astype(jnp.int32)
        rows = normed[order]
        gate_matrix = lax.dynamic_slice_in_dim(w_gate, expert * block_width, block_width, 2).transpose(1, 0, 2).reshape(D, FF)
        up_matrix = lax.dynamic_slice_in_dim(w_up, expert * block_width, block_width, 2).transpose(1, 0, 2).reshape(D, FF)
        down_matrix = lax.dynamic_slice_in_dim(w_down, expert * block_width, block_width, 1).reshape(FF, D)
        gate = jnp.dot(rows, gate_matrix, preferred_element_type=jnp.float32)
        up = jnp.dot(rows, up_matrix, preferred_element_type=jnp.float32)
        hidden = (jax.nn.silu(gate) * up).astype(jnp.bfloat16)
        expert_out = jnp.dot(hidden, down_matrix, preferred_element_type=jnp.float32)
        return total.at[order].add(coef[order][:, None] * expert_out)
    mixture = lax.fori_loop(0, E, add_expert, jnp.zeros((SEQUENCE_TOKENS, D), jnp.float32))
    return (stream + mixture).astype(jnp.bfloat16)
```

```python
import functools

import jax
import jax.numpy as jnp
from jax import lax
from jax.experimental import pallas as pl
from jax.experimental.pallas import tpu as pltpu
from jax.sharding import PartitionSpec as P

QUERY_HEAD_COUNT = 32
KEY_VALUE_HEADS = 8
HEAD_DIMENSION = 128
E = 8
MOSTB = 32


neg_fill = -1e30
norm_eps = 1e-05


def doc_index(positions, doc_ends):
    return jnp.sum((positions[:, None] >= doc_ends[None, :]).astype(jnp.int32), axis=1)


def running_sum(counts):
    order = jnp.arange(counts.shape[0], dtype=jnp.int32)
    upto = (order[None, :] <= order[:, None]).reshape(order.shape * 2 + (1,) * (counts.ndim - 1))
    return jnp.sum(jnp.where(upto, counts[None], 0), axis=1)


def rms_scale(stream, norm_gain):
    meansq = jnp.mean(stream * stream, axis=1, keepdims=True)
    return (stream * lax.rsqrt(meansq + norm_eps) * norm_gain).astype(jnp.bfloat16)


def per_device(
    query,
    keys,
    values,
    residual,
    out_weight,
    norm_gain,
    expert_ids,
    gate_codes,
    doc_lengths,
    w_gate,
    w_up,
    w_down,
):
    block_rows = query.shape[0]
    head_size = HEAD_DIMENSION
    q_heads = query.shape[1] // head_size
    kv_heads = keys.shape[1] // head_size
    group_width = QUERY_HEAD_COUNT // KEY_VALUE_HEADS
    width = residual.shape[1]
    sec_count = lax.axis_size("sec")
    rank_count = lax.axis_size("tp") * lax.axis_size("pp")
    pp_index = lax.axis_index("pp")
    rank_index = lax.axis_index("tp") * lax.axis_size("pp") + pp_index
    own_rows = block_rows // rank_count
    own_start = rank_index * own_rows
    doc_ends = running_sum(doc_lengths)
    query_pos = lax.axis_index("sec") * block_rows + jnp.arange(block_rows, dtype=jnp.int32)
    query_doc = doc_index(query_pos, doc_ends)
    kv_pick = (pp_index * q_heads + jnp.arange(q_heads, dtype=jnp.int32)) // group_width
    query_heads = query.reshape(block_rows, q_heads, head_size)
    scale = head_size ** (-0.5)
    run_max = jnp.full((q_heads, block_rows), neg_fill, jnp.float32)
    key_piece = lax.all_gather(keys, "sec", axis=0, tiled=True)
    value_piece = lax.all_gather(values, "sec", axis=0, tiled=True)
    count = key_piece.shape[0]
    key_heads = jnp.take(key_piece.reshape(count, kv_heads, head_size), kv_pick, axis=1)
    value_heads = jnp.take(value_piece.reshape(count, kv_heads, head_size), kv_pick, axis=1)
    scores = (
        jnp.einsum("qhd,khd->hqk", query_heads, key_heads, preferred_element_type=jnp.float32)
        * scale
    )
    key_pos = jnp.arange(count, dtype=jnp.int32)
    allowed = (key_pos[None, :] <= query_pos[:, None]) & (
        doc_index(key_pos, doc_ends)[None, :] == query_doc[:, None]
    )
    scores = jnp.where(allowed[None], scores, neg_fill)
    new_max = jnp.maximum(run_max, jnp.max(scores, axis=2))
    probs = jnp.where(allowed[None], jnp.exp(scores - new_max[:, :, None]), 0.0)
    run_total = jnp.sum(probs, axis=2)
    run_acc = jnp.einsum(
        "hqk,khd->hqd", probs.astype(jnp.bfloat16), value_heads, preferred_element_type=jnp.float32
    )
    run_max, run_total, run_acc = (new_max, run_total, run_acc)
    attended = (
        (run_acc / run_total[:, :, None])
        .transpose(1, 0, 2)
        .reshape(block_rows, q_heads * head_size)
        .astype(jnp.bfloat16)
    )
    rows_in = attended
    mixed_own = lax.psum_scatter(
        jnp.dot(rows_in, out_weight, preferred_element_type=jnp.float32).astype(jnp.bfloat16),
        ("tp", "pp"),
        scatter_dimension=0,
        tiled=True,
    ).astype(jnp.float32)
    stream_own = (
        lax.dynamic_slice_in_dim(residual, own_start, own_rows, 0).astype(jnp.float32) + mixed_own
    )
    normed = lax.all_gather(rms_scale(stream_own, norm_gain), ("tp", "pp"), axis=0, tiled=True)
    capacity = MOSTB
    experts_here = max(1, E // sec_count)
    halves = max(1, sec_count // E)
    route_hits = (expert_ids[:, :, None] == jnp.arange(E, dtype=jnp.int32)[None, None, :]).astype(
        jnp.int32
    )
    member = jnp.sum(route_hits, axis=1)
    slots = running_sum(member) - 1
    slot_pick = jnp.sum(route_hits * slots[:, None, :], axis=2)
    codes = gate_codes.astype(jnp.float32)
    shares = codes / jnp.sum(codes, axis=1, keepdims=True)
    slot_range = jnp.arange(capacity, dtype=jnp.int32)
    select = (
        (slots.T[:, None, :] == slot_range[None, :, None]) & (member.T[:, None, :] == 1)
    ).astype(jnp.bfloat16)
    gate_local = w_gate[0].reshape(width, experts_here, -1)
    up_local = w_up[0].reshape(width, experts_here, -1)
    down_local = w_down[0].reshape(experts_here, -1, width)
    packed = jnp.einsum("ecr,rd->ecd", select, normed, preferred_element_type=jnp.float32).astype(
        jnp.bfloat16
    )
    packed = jnp.repeat(packed, halves, axis=0)
    rows_in = lax.all_to_all(
        packed.reshape(sec_count, experts_here, capacity, normed.shape[1]),
        "sec",
        split_axis=0,
        concat_axis=0,
        tiled=True,
    )
    gate = jnp.einsum("sxmd,dxf->sxmf", rows_in, gate_local, preferred_element_type=jnp.float32)
    up = jnp.einsum("sxmd,dxf->sxmf", rows_in, up_local, preferred_element_type=jnp.float32)
    hidden = (jax.nn.silu(gate) * up).astype(jnp.bfloat16)
    partial_out = jnp.einsum(
        "sxmf,xfd->sxmd", hidden, down_local, preferred_element_type=jnp.float32
    )
    returned = lax.all_to_all(
        partial_out.astype(jnp.bfloat16), "sec", split_axis=0, concat_axis=0, tiled=True
    ).astype(partial_out.dtype)
    flat_parts = returned.reshape(sec_count * experts_here * capacity, width)
    half_range = jnp.arange(halves, dtype=jnp.int32)
    top_count = expert_ids.shape[1]
    index = ((expert_ids * halves)[:, :, None] + half_range[None, None, :]) * capacity + slot_pick[
        :, :, None
    ]
    picked = jnp.take(flat_parts, index.reshape(-1), axis=0).reshape(
        own_rows * lax.axis_size(("tp", "pp")), top_count, halves, width
    )
    mixture_own = lax.psum_scatter(
        jnp.sum(picked * shares[:, :, None, None], axis=(1, 2)).astype(jnp.bfloat16),
        ("tp", "pp"),
        scatter_dimension=0,
        tiled=True,
    ).astype(jnp.float32)
    return (stream_own + mixture_own).astype(jnp.bfloat16)


MESH = pl.DeviceIdType.MESH
COLUMN_CHUNKS = 4
WEIGHT_CHUNKS = 4


def rcopy(src, dst, send_sem, recv_sem, device):
    return pltpu.make_async_remote_copy(
        src_ref=src,
        dst_ref=dst,
        send_sem=send_sem,
        recv_sem=recv_sem,
        device_id=device,
        device_id_type=MESH,
    )


def layer_kernel(
    n_sec,
    docs,
    lengths,
    query,
    keys,
    values,
    residual,
    out_weight,
    norm_gain,
    ids,
    codes,
    w_gate,
    w_up,
    w_down,
    out,
    qv,
    kv,
    vv,
    attv,
    wov,
    resv,
    gainv,
    idsv,
    codesv,
    routev,
    wgv,
    wuv,
    wdv,
    part,
    mixin,
    stream,
    nall,
    packed,
    hidden,
    pickv,
    pickt,
    sharev,
    pout,
    r1,
    acc,
    x_out,
    r2,
    z_out,
    r3,
    load_sem,
    w_sem,
    kv_send,
    kv_recv,
    route_send,
    route_recv,
    mix_send,
    mix_recv,
    nz_send,
    nz_recv,
    nx_send,
    nx_recv,
    nc_send,
    nc_recv,
    c1_send,
    c1_recv,
    x2_send,
    x2_recv,
    z3_send,
    z3_recv,
):
    f32, bf16 = jnp.float32, jnp.bfloat16
    me, tx, core = lax.axis_index("sec"), lax.axis_index("tp"), lax.axis_index("pp")
    rank = tx * 2 + core
    rows, width = residual.shape
    own = rows // 4
    kv_width = kv.shape[1]
    tokens = n_sec * rows
    half, quarter = tokens // 2, tokens // 4
    x_peer, c_peer = {"tp": 1 - tx}, {"pp": 1 - core}
    d_peer = {"tp": 1 - tx, "pp": 1 - core}
    sec_of = lambda d: lax.rem(me + d, n_sec)
    longest = tokens // 2
    reach = min(n_sec - 1, pl.cdiv(longest - 1, rows))

    def nearest(visit):
        for distance in range(1, n_sec):
            for z in (me + distance, me - distance):
                pl.when((z >= 0) & (z < n_sec))(functools.partial(visit, z))


    def load(src, dst, i):
        copy = pltpu.make_async_copy(src, dst, load_sem.at[i])
        copy.start()
        return copy

    barrier = pltpu.get_barrier_semaphore()
    for d in range(1, n_sec):
        pl.semaphore_signal(barrier, inc=1, device_id={"sec": sec_of(d)}, device_id_type=MESH)
    for peer in (x_peer, c_peer, d_peer):
        pl.semaphore_signal(barrier, inc=1, device_id=peer, device_id_type=MESH)

    columns = pl.ds(pl.multiple_of(core * kv_width, 128), kv_width)
    block = lambda z: pl.ds(pl.multiple_of(z * rows, rows), rows)
    load_k = load(keys.at[:, columns], kv.at[block(me), :], 0)
    load_v = load(values.at[:, columns], vv.at[block(me), :], 1)
    load_ids = load(ids, idsv, 2)
    load_codes = load(codes, codesv, 7)
    load_q = load(query, qv, 3)
    load_wo = load(out_weight, wov, 4)
    load_res = load(residual.at[pl.ds(pl.multiple_of(rank * own, own), own), :], resv, 5)
    load_gain = load(norm_gain, gainv, 6)
    weight_loads = []
    for which, (src, dst) in enumerate(((w_gate, wgv), (w_up, wuv), (w_down, wdv))):
        span = dst.shape[1] // WEIGHT_CHUNKS
        loads = []
        for i in range(WEIGHT_CHUNKS):
            piece = pl.ds(i * span, span)
            copy = pltpu.make_async_copy(
                src.at[0, :, piece], dst.at[:, piece], w_sem.at[which, i]
            )
            loads.append(copy)
        weight_loads.append(loads)

    for z in range(n_sec):

        @pl.when((z > me) | (z < me - reach))
        def _():
            kv[z * rows : (z + 1) * rows, :] = jnp.zeros((rows, kv_width), bf16)
            vv[z * rows : (z + 1) * rows, :] = jnp.zeros((rows, kv_width), bf16)

    pl.semaphore_wait(barrier, n_sec + 2)

    def kv_copy(which, ref, d, z, device, src=None):
        return rcopy(
            ref.at[block(z), :] if src is None else src.at[:, columns],
            ref.at[block(z), :],
            kv_send.at[which, d],
            kv_recv.at[which, z],
            device,
        )

    for which, (ref, src) in enumerate(((kv, keys), (vv, values))):
        for d in range(1, reach + 1):

            @pl.when(me + d < n_sec)
            def _():
                kv_copy(which, ref, d, me, {"sec": sec_of(d)}, src).start()

    load_ids.wait()
    load_codes.wait()
    given = jnp.concatenate(
        [idsv[...].astype(f32), codesv[...].astype(f32), jnp.zeros((4, rows), f32)], axis=0
    )
    lane = lax.broadcasted_iota(jnp.int32, (rows, tokens), 1)
    row_of = (
        lax.rem(lane // quarter, 2) * (2 * own) + lane // half * own + lax.rem(lane, own)
    )
    here_z = lax.rem(lane, quarter) // own == me
    spread = jnp.where(
        here_z & (row_of == lax.broadcasted_iota(jnp.int32, (rows, tokens), 0)), 1.0, 0.0
    )
    routev[me] = jnp.dot(given.astype(bf16), spread.astype(bf16), preferred_element_type=f32)

    def route_copy(d, z):
        return rcopy(
            routev.at[z], routev.at[z], route_send.at[d], route_recv.at[z], {"sec": sec_of(d)}
        )

    for d in range(1, n_sec):
        route_copy(d, me).start()

    for i in range(WEIGHT_CHUNKS):
        weight_loads[0][i].start()
        weight_loads[1][i].start()

    load_q.wait()
    shape = (rows, tokens)
    query_pos = lax.broadcasted_iota(jnp.int32, shape, 0) + me * rows
    key_pos = lax.broadcasted_iota(jnp.int32, shape, 1)
    query_doc = jnp.zeros(shape, jnp.int32)
    key_doc = jnp.zeros(shape, jnp.int32)
    end = jnp.int32(0)
    for i in range(docs):
        end = end + lengths[i]
        query_doc += (query_pos >= end).astype(jnp.int32)
        key_doc += (key_pos >= end).astype(jnp.int32)
    allowed = jnp.where((key_pos <= query_pos) & (query_doc == key_doc), 1.0, 0.0)
    size = HEAD_DIMENSION
    group_width = QUERY_HEAD_COUNT // KEY_VALUE_HEADS
    allowed = jnp.concatenate([allowed] * group_width, axis=0) > 0.5

    for z in range(n_sec - 1):

        @pl.when((z < me) & (z >= me - reach))
        def _():
            kv_copy(0, kv, 1, z, {"sec": sec_of(1)}).wait_recv()
            kv_copy(1, vv, 1, z, {"sec": sec_of(1)}).wait_recv()

    load_k.wait()
    load_v.wait()
    for g in range(kv_width // size):
        heads = range(g * group_width, (g + 1) * group_width)
        q = jnp.concatenate([qv[:, h * size : (h + 1) * size] for h in heads], axis=0)
        k = kv[:, g * size : (g + 1) * size]
        v = vv[:, g * size : (g + 1) * size]
        scores = lax.dot_general(
            q, k, (((1,), (1,)), ((), ())), preferred_element_type=f32
        ) * (size ** (-0.5))
        scores = jnp.where(allowed, scores, neg_fill)
        top = jnp.max(scores, axis=1, keepdims=True)
        probs = jnp.where(allowed, jnp.exp(scores - top), 0.0)
        total = jnp.sum(probs, axis=1, keepdims=True)
        mixed = jnp.dot(probs.astype(bf16), v, preferred_element_type=f32) / total
        mixed = mixed.astype(bf16)
        for i, h in enumerate(heads):
            attv[:, h * size : (h + 1) * size] = mixed[i * rows : (i + 1) * rows, :]

    load_wo.wait()
    part[...] = jnp.dot(attv[...], wov[...], preferred_element_type=f32).astype(bf16)

    own_at = lambda r: pl.ds(pl.multiple_of(r * own, own), own)
    mix_sends = []
    for i, (peer, target) in enumerate(
        (
            (d_peer, (1 - tx) * 2 + 1 - core),
            (x_peer, (1 - tx) * 2 + core),
            (c_peer, tx * 2 + 1 - core),
        )
    ):
        copy = rcopy(part.at[own_at(target), :], mixin.at[i], mix_send.at[i], mix_recv.at[i], peer)
        copy.start()
        mix_sends.append(copy)
    for copy in weight_loads[2]:
        copy.start()

    for d in range(1, n_sec):
        route_copy(d, sec_of(d)).wait_recv()
    facts = routev[0]
    for z in range(1, n_sec):
        facts = facts + routev[z]
    here = E // n_sec
    capacity = n_sec * MOSTB
    first, second = facts[0:1, :], facts[1:2, :]
    code_a, code_b = facts[2:3, :], facts[3:4, :]
    base = (me * here).astype(f32)
    local = lax.broadcasted_iota(jnp.int32, (8, tokens), 0).astype(f32) + base
    member = jnp.where((first == local) | (second == local), 1.0, 0.0)
    before = jnp.where(
        lax.broadcasted_iota(jnp.int32, (tokens, tokens), 0)
        < lax.broadcasted_iota(jnp.int32, (tokens, tokens), 1),
        1.0,
        0.0,
    ).astype(bf16)
    standing = jnp.dot(member.astype(bf16), before, preferred_element_type=f32)
    slot = lax.broadcasted_iota(jnp.int32, (capacity, tokens), 0).astype(f32)
    picks = []
    for e in range(here):
        pick = jnp.where((standing[e : e + 1, :] == slot) & (member[e : e + 1, :] > 0.5), 1.0, 0.0)
        coef = jnp.where(first == base + e, code_a, 0.0) + jnp.where(second == base + e, code_b, 0.0)
        coef = coef / (code_a + code_b)
        share = jnp.sum(pick * coef, axis=1, keepdims=True)
        sharev[e * capacity : (e + 1) * capacity, :] = jnp.broadcast_to(share, (capacity, 128))
        picks.append(pick)
    pick = jnp.concatenate(picks, axis=0)
    pickv[...] = pick.astype(bf16)
    pickt[...] = jnp.transpose(pick).astype(bf16)

    load_res.wait()
    load_gain.wait()
    for copy in mix_sends:
        copy.wait_recv()
    total = part[own_at(rank), :].astype(f32)
    for i in range(3):
        total = total + mixin[i].astype(f32)
    total = total + resv[...].astype(f32)
    stream[...] = total
    meansq = jnp.mean(total * total, axis=1, keepdims=True)
    spot = lambda c, x, z: pl.ds(
        pl.multiple_of(c * half + x * quarter + z * own, own), own
    )
    mine = spot(core, tx, me)
    nall[mine, :] = (total * lax.rsqrt(meansq + norm_eps) * gainv[...]).astype(bf16)

    def nz_copy(to, z):
        at = nall.at[spot(core, tx, z), :]
        return rcopy(at, at, nz_send.at[to], nz_recv.at[z], {"sec": to})

    def nx_copy(x, z):
        at = nall.at[spot(core, x, z), :]
        return rcopy(at, at, nx_send.at[z], nx_recv.at[z], x_peer)

    def nc_copy(c, x, z):
        at = nall.at[spot(c, x, z), :]
        return rcopy(at, at, nc_send.at[x, z], nc_recv.at[x, z], c_peer)

    def onward(z):
        nx_copy(tx, z).start()
        nc_copy(core, tx, z).start()

    def from_z(z):
        nz_copy(z, z).wait_recv()
        onward(z)

    def from_x(z):
        nx_copy(1 - tx, z).wait_recv()
        nc_copy(core, 1 - tx, z).start()

    nearest(lambda z: nz_copy(z, me).start())
    onward(me)
    nearest(from_z)
    from_x(me)
    nearest(from_x)
    for x in (tx, 1 - tx):
        for z in range(n_sec):
            nc_copy(1 - core, x, z).wait_recv()

    packed[...] = jnp.dot(pickv[...], nall[...], preferred_element_type=f32).astype(bf16)

    for copy in weight_loads[0] + weight_loads[1]:
        copy.wait()
    units = wgv.shape[1] // here
    tile = units
    tiles = units // tile

    def expand(j, carry):
        e, f = j // tiles, lax.rem(j, tiles)
        slots = pl.ds(pl.multiple_of(e * capacity, capacity), capacity)
        at = pl.ds(pl.multiple_of(j * tile, tile), tile)
        x = packed[slots, :]
        gate = jnp.dot(x, wgv[:, at], preferred_element_type=f32)
        up = jnp.dot(x, wuv[:, at], preferred_element_type=f32)
        act = gate / (1.0 + jnp.exp(-gate)) * up
        hidden[slots, pl.ds(pl.multiple_of(f * tile, tile), tile)] = act.astype(bf16)
        return carry

    lax.fori_loop(0, here * tiles, expand, 0)

    for copy in weight_loads[2]:
        copy.wait()
    span = width // COLUMN_CHUNKS
    sub = span

    def shrink(c):
        def piece(i, carry):
            at = pl.ds(pl.multiple_of(c * span + i * sub, sub), sub)
            outs = []
            for e in range(here):
                slots = slice(e * capacity, (e + 1) * capacity)
                y = jnp.dot(
                    hidden[slots, :],
                    wdv[e * units : (e + 1) * units, at],
                    preferred_element_type=f32,
                )
                outs.append((y * sharev[slots, 0:1]).astype(bf16))
            y = jnp.concatenate(outs, axis=0)
            pout[:, at] = jnp.dot(pickt[...], y, preferred_element_type=f32).astype(bf16)
            return carry

        lax.fori_loop(0, span // sub, piece, 0)

    half_at = lambda c: pl.ds(pl.multiple_of(c * half, half), half)
    quarter_at = lambda x: pl.ds(pl.multiple_of(x * quarter, quarter), quarter)

    def c1_copy(c):
        at = pl.ds(c * span, span)
        return rcopy(
            pout.at[half_at(1 - core), at], r1.at[:, at], c1_send.at[c], c1_recv.at[c], c_peer
        )

    def x2_copy(c):
        at = pl.ds(c * span, span)
        return rcopy(x_out.at[:, at], r2.at[:, at], x2_send.at[c], x2_recv.at[c], x_peer)

    def z3_copy(c, d, z, device):
        at = pl.ds(c * span, span)
        return rcopy(
            z_out.at[own_at(sec_of(d)), at],
            r3.at[own_at(z), at],
            z3_send.at[c, d],
            z3_recv.at[c, z],
            device,
        )

    def cross_core(c):
        at = slice(c * span, (c + 1) * span)
        c1_copy(c).wait_recv()
        other = pl.ds(pl.multiple_of(core * half + (1 - tx) * quarter, quarter), quarter)
        same = pl.ds(pl.multiple_of(core * half + tx * quarter, quarter), quarter)
        x_out[:, at] = (
            pout[other, at].astype(f32) + r1[quarter_at(1 - tx), at].astype(f32)
        ).astype(bf16)
        x2_copy(c).start()
        acc[:, at] = pout[same, at].astype(f32) + r1[quarter_at(tx), at].astype(f32)

    def cross_x(c):
        at = slice(c * span, (c + 1) * span)
        x2_copy(c).wait_recv()
        total = acc[:, at] + r2[:, at].astype(f32)
        acc[:, at] = total
        z_out[:, at] = total.astype(bf16)
        for d in range(n_sec - 1, 0, -1):
            z3_copy(c, d, me, {"sec": sec_of(d)}).start()

    def cross_z(c):
        at = slice(c * span, (c + 1) * span)
        total = stream[:, at] + acc[own_at(me), at]
        for d in range(1, n_sec):
            z = sec_of(d)
            z3_copy(c, d, z, {"sec": z}).wait_recv()
            total = total + r3[own_at(z), at].astype(f32)
        out[:, at] = total.astype(bf16)

    for c in range(COLUMN_CHUNKS):
        shrink(c)
        c1_copy(c).start()
        if c:
            cross_core(c - 1)
    cross_core(COLUMN_CHUNKS - 1)
    for c in range(COLUMN_CHUNKS):
        cross_x(c)
    for c in range(COLUMN_CHUNKS):
        cross_z(c)

    for which, ref in enumerate((kv, vv)):
        for d in range(1, reach + 1):

            @pl.when(me + d < n_sec)
            def _():
                kv_copy(which, ref, d, me, {"sec": sec_of(d)}).wait_send()

    for d in range(1, n_sec):
        route_copy(d, me).wait_send()
    for copy in mix_sends:
        copy.wait_send()
    nearest(lambda z: nz_copy(z, me).wait_send())
    for z in range(n_sec):
        nx_copy(tx, z).wait_send()
        for x in (tx, 1 - tx):
            nc_copy(core, x, z).wait_send()
    for c in range(COLUMN_CHUNKS):
        c1_copy(c).wait_send()
        x2_copy(c).wait_send()
        for d in range(1, n_sec):
            z3_copy(c, d, me, {"sec": sec_of(d)}).wait_send()


def fused_device(
    query,
    keys,
    values,
    residual,
    out_weight,
    norm_gain,
    expert_ids,
    gate_codes,
    doc_lengths,
    w_gate,
    w_up,
    w_down,
):
    n_sec = lax.axis_size("sec")
    rows, width = residual.shape
    own = rows // 4
    tokens = n_sec * rows
    here = E // n_sec
    slots = here * n_sec * MOSTB
    kv_width = query.shape[1] * KEY_VALUE_HEADS // QUERY_HEAD_COUNT
    f32, bf16 = jnp.float32, jnp.bfloat16
    V, dma = pltpu.VMEM, pltpu.SemaphoreType.DMA
    anywhere = pl.BlockSpec(memory_space=pl.ANY)
    return pl.pallas_call(
        functools.partial(layer_kernel, n_sec, doc_lengths.shape[0]),
        out_shape=pltpu.VMEM((own, width), bf16),
        in_specs=[pl.BlockSpec(memory_space=pltpu.SMEM)] + [anywhere] * 11,
        out_specs=pl.BlockSpec(memory_space=pltpu.VMEM),
        scratch_shapes=[
            V(query.shape, bf16),
            V((tokens, kv_width), bf16),
            V((tokens, kv_width), bf16),
            V(query.shape, bf16),
            V(out_weight.shape, bf16),
            V((own, width), bf16),
            V((1, width), f32),
            V(expert_ids.shape[::-1], jnp.int32),
            V(gate_codes.shape[::-1], jnp.int32),
            V((n_sec, 8, tokens), f32),
            V(w_gate.shape[1:], bf16),
            V(w_up.shape[1:], bf16),
            V(w_down.shape[1:], bf16),
            V((rows, width), bf16),
            V((3, own, width), bf16),
            V((own, width), f32),
            V((tokens, width), bf16),
            V((slots, width), bf16),
            V((slots, w_gate.shape[2] // here), bf16),
            V((slots, tokens), bf16),
            V((tokens, slots), bf16),
            V((slots, 128), f32),
            V((tokens, width), bf16),
            V((tokens // 2, width), bf16),
            V((tokens // 4, width), f32),
            V((tokens // 4, width), bf16),
            V((tokens // 4, width), bf16),
            V((tokens // 4, width), bf16),
            V((tokens // 4, width), bf16),
            dma((8,)),
            dma((3, WEIGHT_CHUNKS)),
            dma((2, n_sec)),
            dma((2, n_sec)),
            dma((n_sec,)),
            dma((n_sec,)),
            dma((3,)),
            dma((3,)),
            dma((n_sec,)),
            dma((n_sec,)),
            dma((n_sec,)),
            dma((n_sec,)),
            dma((2, n_sec)),
            dma((2, n_sec)),
            dma((COLUMN_CHUNKS,)),
            dma((COLUMN_CHUNKS,)),
            dma((COLUMN_CHUNKS,)),
            dma((COLUMN_CHUNKS,)),
            dma((COLUMN_CHUNKS, n_sec)),
            dma((COLUMN_CHUNKS, n_sec)),
        ],
        compiler_params=pltpu.CompilerParams(
            collective_id=0, has_side_effects=True, vmem_limit_bytes=66900000
        ),
    )(
        doc_lengths,
        query,
        keys,
        values,
        residual,
        out_weight,
        norm_gain.reshape(1, width),
        expert_ids.T,
        gate_codes.T,
        w_gate,
        w_up,
        w_down,
    )


def whole_in_vmem(mesh):
    shape = mesh.shape
    return shape["tp"] == 2 and shape["pp"] == 2 and shape["sec"] > 1 and E % shape["sec"] == 0


def solution(mesh):
    in_specs = (
        P(("groups", "sec"), ("tp", "pp")),
        P(("groups", "sec"), "tp"),
        P(("groups", "sec"), "tp"),
        P(("groups", "sec"), None),
        P(("tp", "pp"), None),
        P(),
        P(("groups", "sec"), None),
        P(("groups", "sec"), None),
        P("groups"),
        P(("tp", "pp"), None, "sec"),
        P(("tp", "pp"), None, "sec"),
        P(("tp", "pp"), "sec", None),
    )
    out_specs = P(("groups", "sec", "tp", "pp"), None)
    return jax.shard_map(
        fused_device if whole_in_vmem(mesh) else per_device,
        mesh=mesh,
        in_specs=in_specs,
        out_specs=out_specs,
        check_vma=False,
    )
```

```python
import functools

import jax
import jax.numpy as jnp
from jax import lax
from jax.experimental import pallas as pl
from jax.experimental.pallas import tpu as pltpu
from jax.sharding import PartitionSpec as P

QUERY_HEAD_COUNT = 32
KEY_VALUE_HEADS = 8
HEAD_DIMENSION = 128
E = 8
MOSTB = 32


neg_fill = -1e30
norm_eps = 1e-05


def doc_index(positions, doc_ends):
    return jnp.sum((positions[:, None] >= doc_ends[None, :]).astype(jnp.int32), axis=1)


def running_sum(counts):
    order = jnp.arange(counts.shape[0], dtype=jnp.int32)
    upto = (order[None, :] <= order[:, None]).reshape(order.shape * 2 + (1,) * (counts.ndim - 1))
    return jnp.sum(jnp.where(upto, counts[None], 0), axis=1)


def rms_scale(stream, norm_gain):
    meansq = jnp.mean(stream * stream, axis=1, keepdims=True)
    return (stream * lax.rsqrt(meansq + norm_eps) * norm_gain).astype(jnp.bfloat16)


def per_device(
    query,
    keys,
    values,
    residual,
    out_weight,
    norm_gain,
    expert_ids,
    gate_codes,
    doc_lengths,
    w_gate,
    w_up,
    w_down,
):
    block_rows = query.shape[0]
    head_size = HEAD_DIMENSION
    q_heads = query.shape[1] // head_size
    kv_heads = keys.shape[1] // head_size
    group_width = QUERY_HEAD_COUNT // KEY_VALUE_HEADS
    width = residual.shape[1]
    sec_count = lax.axis_size("sec")
    rank_count = lax.axis_size("tp") * lax.axis_size("pp")
    pp_index = lax.axis_index("pp")
    rank_index = lax.axis_index("tp") * lax.axis_size("pp") + pp_index
    own_rows = block_rows // rank_count
    own_start = rank_index * own_rows
    doc_ends = running_sum(doc_lengths)
    query_pos = lax.axis_index("sec") * block_rows + jnp.arange(block_rows, dtype=jnp.int32)
    query_doc = doc_index(query_pos, doc_ends)
    kv_pick = (pp_index * q_heads + jnp.arange(q_heads, dtype=jnp.int32)) // group_width
    query_heads = query.reshape(block_rows, q_heads, head_size)
    scale = head_size ** (-0.5)
    run_max = jnp.full((q_heads, block_rows), neg_fill, jnp.float32)
    key_piece = lax.all_gather(keys, "sec", axis=0, tiled=True)
    value_piece = lax.all_gather(values, "sec", axis=0, tiled=True)
    count = key_piece.shape[0]
    key_heads = jnp.take(key_piece.reshape(count, kv_heads, head_size), kv_pick, axis=1)
    value_heads = jnp.take(value_piece.reshape(count, kv_heads, head_size), kv_pick, axis=1)
    scores = (
        jnp.einsum("qhd,khd->hqk", query_heads, key_heads, preferred_element_type=jnp.float32)
        * scale
    )
    key_pos = jnp.arange(count, dtype=jnp.int32)
    allowed = (key_pos[None, :] <= query_pos[:, None]) & (
        doc_index(key_pos, doc_ends)[None, :] == query_doc[:, None]
    )
    scores = jnp.where(allowed[None], scores, neg_fill)
    new_max = jnp.maximum(run_max, jnp.max(scores, axis=2))
    probs = jnp.where(allowed[None], jnp.exp(scores - new_max[:, :, None]), 0.0)
    run_total = jnp.sum(probs, axis=2)
    run_acc = jnp.einsum(
        "hqk,khd->hqd", probs.astype(jnp.bfloat16), value_heads, preferred_element_type=jnp.float32
    )
    run_max, run_total, run_acc = (new_max, run_total, run_acc)
    attended = (
        (run_acc / run_total[:, :, None])
        .transpose(1, 0, 2)
        .reshape(block_rows, q_heads * head_size)
        .astype(jnp.bfloat16)
    )
    rows_in = attended
    mixed_own = lax.psum_scatter(
        jnp.dot(rows_in, out_weight, preferred_element_type=jnp.float32).astype(jnp.bfloat16),
        ("tp", "pp"),
        scatter_dimension=0,
        tiled=True,
    ).astype(jnp.float32)
    stream_own = (
        lax.dynamic_slice_in_dim(residual, own_start, own_rows, 0).astype(jnp.float32) + mixed_own
    )
    normed = lax.all_gather(rms_scale(stream_own, norm_gain), ("tp", "pp"), axis=0, tiled=True)
    capacity = MOSTB
    experts_here = max(1, E // sec_count)
    halves = max(1, sec_count // E)
    route_hits = (expert_ids[:, :, None] == jnp.arange(E, dtype=jnp.int32)[None, None, :]).astype(
        jnp.int32
    )
    member = jnp.sum(route_hits, axis=1)
    slots = running_sum(member) - 1
    slot_pick = jnp.sum(route_hits * slots[:, None, :], axis=2)
    codes = gate_codes.astype(jnp.float32)
    shares = codes / jnp.sum(codes, axis=1, keepdims=True)
    slot_range = jnp.arange(capacity, dtype=jnp.int32)
    select = (
        (slots.T[:, None, :] == slot_range[None, :, None]) & (member.T[:, None, :] == 1)
    ).astype(jnp.bfloat16)
    gate_local = w_gate[0].reshape(width, experts_here, -1)
    up_local = w_up[0].reshape(width, experts_here, -1)
    down_local = w_down[0].reshape(experts_here, -1, width)
    packed = jnp.einsum("ecr,rd->ecd", select, normed, preferred_element_type=jnp.float32).astype(
        jnp.bfloat16
    )
    packed = jnp.repeat(packed, halves, axis=0)
    rows_in = lax.all_to_all(
        packed.reshape(sec_count, experts_here, capacity, normed.shape[1]),
        "sec",
        split_axis=0,
        concat_axis=0,
        tiled=True,
    )
    gate = jnp.einsum("sxmd,dxf->sxmf", rows_in, gate_local, preferred_element_type=jnp.float32)
    up = jnp.einsum("sxmd,dxf->sxmf", rows_in, up_local, preferred_element_type=jnp.float32)
    hidden = (jax.nn.silu(gate) * up).astype(jnp.bfloat16)
    partial_out = jnp.einsum(
        "sxmf,xfd->sxmd", hidden, down_local, preferred_element_type=jnp.float32
    )
    returned = lax.all_to_all(
        partial_out.astype(jnp.bfloat16), "sec", split_axis=0, concat_axis=0, tiled=True
    ).astype(partial_out.dtype)
    flat_parts = returned.reshape(sec_count * experts_here * capacity, width)
    half_range = jnp.arange(halves, dtype=jnp.int32)
    top_count = expert_ids.shape[1]
    index = ((expert_ids * halves)[:, :, None] + half_range[None, None, :]) * capacity + slot_pick[
        :, :, None
    ]
    picked = jnp.take(flat_parts, index.reshape(-1), axis=0).reshape(
        own_rows * lax.axis_size(("tp", "pp")), top_count, halves, width
    )
    mixture_own = lax.psum_scatter(
        jnp.sum(picked * shares[:, :, None, None], axis=(1, 2)).astype(jnp.bfloat16),
        ("tp", "pp"),
        scatter_dimension=0,
        tiled=True,
    ).astype(jnp.float32)
    return (stream_own + mixture_own).astype(jnp.bfloat16)


MESH = pl.DeviceIdType.MESH
LANES = 128
GATHER_CHUNKS = 4
RETURN_EIGHTHS = (2, 2, 2, 2)
WEIGHT_CHUNKS = 4


def rcopy(src, dst, send_sem, recv_sem, device):
    return pltpu.make_async_remote_copy(
        src_ref=src,
        dst_ref=dst,
        send_sem=send_sem,
        recv_sem=recv_sem,
        device_id=device,
        device_id_type=MESH,
    )


def layer_kernel(
    n_sec,
    docs,
    lengths,
    query,
    keys,
    values,
    residual,
    out_weight,
    norm_gain,
    ids,
    codes,
    w_gate,
    w_up,
    w_down,
    out,
    qv,
    kv,
    vv,
    attv,
    resv,
    gainv,
    idsv,
    codesv,
    routev,
    wgv,
    wuv,
    wdv,
    part,
    mixin,
    stream,
    nall,
    packed,
    gacc,
    uacc,
    hidden,
    pickv,
    pickt,
    sharev,
    r1,
    x_out,
    r2,
    z_out,
    r3,
    load_sem,
    w_sem,
    kv_send,
    kv_recv,
    route_send,
    route_recv,
    mix_send,
    mix_recv,
    nz_send,
    nz_recv,
    nx_send,
    nx_recv,
    nc_send,
    nc_recv,
    c1_send,
    c1_recv,
    x2_send,
    x2_recv,
    z3_send,
    z3_recv,
):
    f32, bf16 = jnp.float32, jnp.bfloat16
    me, tx, core = lax.axis_index("sec"), lax.axis_index("tp"), lax.axis_index("pp")
    rank = tx * 2 + core
    rows, width = residual.shape
    own = rows // 4
    kv_width = kv.shape[1]
    tokens = n_sec * rows
    half, quarter = tokens // 2, tokens // 4
    x_peer, c_peer = {"tp": 1 - tx}, {"pp": 1 - core}
    d_peer = {"tp": 1 - tx, "pp": 1 - core}
    sec_of = lambda d: lax.rem(me + d, n_sec)
    longest = tokens // 2
    reach = min(n_sec - 1, pl.cdiv(longest - 1, rows))

    def nearest(visit):
        for distance in range(1, n_sec):
            for z in (me + distance, me - distance):
                pl.when((z >= 0) & (z < n_sec))(functools.partial(visit, z))


    def load(src, dst, i):
        copy = pltpu.make_async_copy(src, dst, load_sem.at[i])
        copy.start()
        return copy

    barrier = pltpu.get_barrier_semaphore()
    for d in range(1, n_sec):
        pl.semaphore_signal(barrier, inc=1, device_id={"sec": sec_of(d)}, device_id_type=MESH)
    for peer in (x_peer, c_peer, d_peer):
        pl.semaphore_signal(barrier, inc=1, device_id=peer, device_id_type=MESH)

    columns = pl.ds(pl.multiple_of(core * kv_width, 128), kv_width)
    block = lambda z: pl.ds(pl.multiple_of(z * rows, rows), rows)
    load_k = load(keys.at[:, columns], kv.at[block(me), :], 0)
    load_v = load(values.at[:, columns], vv.at[block(me), :], 1)
    load_ids = load(ids, idsv, 2)
    load_codes = load(codes, codesv, 7)
    load_q = load(query, qv, 3)
    wov = wdv.at[pl.ds(0, out_weight.shape[0]), :]
    load_wo = load(out_weight, wov, 4)
    load_res = load(residual.at[pl.ds(pl.multiple_of(rank * own, own), own), :], resv, 5)
    load_gain = load(norm_gain, gainv, 6)
    weight_loads = []
    for which, (src, dst) in enumerate(((w_gate, wgv), (w_up, wuv), (w_down, wdv))):
        span = dst.shape[1] // WEIGHT_CHUNKS
        loads = []
        for i in range(WEIGHT_CHUNKS):
            piece = pl.ds(i * span, span)
            copy = pltpu.make_async_copy(
                src.at[0, :, piece], dst.at[:, piece], w_sem.at[which, i]
            )
            loads.append(copy)
        weight_loads.append(loads)

    for z in range(n_sec):

        @pl.when((z > me) | (z < me - reach))
        def _():
            kv[z * rows : (z + 1) * rows, :] = jnp.zeros((rows, kv_width), bf16)
            vv[z * rows : (z + 1) * rows, :] = jnp.zeros((rows, kv_width), bf16)

    pl.semaphore_wait(barrier, n_sec + 2)

    def kv_copy(which, ref, d, z, device, src=None):
        return rcopy(
            ref.at[block(z), :] if src is None else src.at[:, columns],
            ref.at[block(z), :],
            kv_send.at[which, d],
            kv_recv.at[which, z],
            device,
        )

    for which, (ref, src) in enumerate(((kv, keys), (vv, values))):
        for d in range(1, reach + 1):

            @pl.when(me + d < n_sec)
            def _():
                kv_copy(which, ref, d, me, {"sec": sec_of(d)}, src).start()

    load_ids.wait()
    load_codes.wait()
    given = jnp.concatenate(
        [idsv[...].astype(f32), codesv[...].astype(f32), jnp.zeros((4, rows), f32)], axis=0
    )
    lane = lax.broadcasted_iota(jnp.int32, (rows, tokens), 1)
    row_of = (
        lax.rem(lane // quarter, 2) * (2 * own) + lane // half * own + lax.rem(lane, own)
    )
    here_z = lax.rem(lane, quarter) // own == me
    spread = jnp.where(
        here_z & (row_of == lax.broadcasted_iota(jnp.int32, (rows, tokens), 0)), 1.0, 0.0
    )
    routev[me] = jnp.dot(given.astype(bf16), spread.astype(bf16), preferred_element_type=f32)

    def route_copy(d, z):
        return rcopy(
            routev.at[z], routev.at[z], route_send.at[d], route_recv.at[z], {"sec": sec_of(d)}
        )

    for d in range(1, n_sec):
        route_copy(d, me).start()

    for i in range(WEIGHT_CHUNKS):
        weight_loads[0][i].start()
        weight_loads[1][i].start()

    load_q.wait()
    shape = (rows, tokens)
    query_pos = lax.broadcasted_iota(jnp.int32, shape, 0) + me * rows
    key_pos = lax.broadcasted_iota(jnp.int32, shape, 1)
    query_doc = jnp.zeros(shape, jnp.int32)
    key_doc = jnp.zeros(shape, jnp.int32)
    end = jnp.int32(0)
    for i in range(docs):
        end = end + lengths[i]
        query_doc += (query_pos >= end).astype(jnp.int32)
        key_doc += (key_pos >= end).astype(jnp.int32)
    allowed = jnp.where((key_pos <= query_pos) & (query_doc == key_doc), 1.0, 0.0)
    size = HEAD_DIMENSION
    group_width = QUERY_HEAD_COUNT // KEY_VALUE_HEADS
    allowed = jnp.concatenate([allowed] * group_width, axis=0) > 0.5

    for z in range(n_sec - 1):

        @pl.when((z < me) & (z >= me - reach))
        def _():
            kv_copy(0, kv, 1, z, {"sec": sec_of(1)}).wait_recv()
            kv_copy(1, vv, 1, z, {"sec": sec_of(1)}).wait_recv()

    load_k.wait()
    load_v.wait()
    for g in range(kv_width // size):
        heads = range(g * group_width, (g + 1) * group_width)
        q = jnp.concatenate([qv[:, h * size : (h + 1) * size] for h in heads], axis=0)
        k = kv[:, g * size : (g + 1) * size]
        v = vv[:, g * size : (g + 1) * size]
        scores = lax.dot_general(
            q, k, (((1,), (1,)), ((), ())), preferred_element_type=f32
        ) * (size ** (-0.5))
        scores = jnp.where(allowed, scores, neg_fill)
        top = jnp.max(scores, axis=1, keepdims=True)
        probs = jnp.where(allowed, jnp.exp(scores - top), 0.0)
        total = jnp.sum(probs, axis=1, keepdims=True)
        mixed = jnp.dot(probs.astype(bf16), v, preferred_element_type=f32) / total
        mixed = mixed.astype(bf16)
        for i, h in enumerate(heads):
            attv[:, h * size : (h + 1) * size] = mixed[i * rows : (i + 1) * rows, :]

    load_wo.wait()
    gather_span = width // GATHER_CHUNKS
    own_at = lambda r: pl.ds(pl.multiple_of(r * own, own), own)
    mix_from = (
        (d_peer, (1 - tx) * 2 + 1 - core),
        (x_peer, (1 - tx) * 2 + core),
        (c_peer, tx * 2 + 1 - core),
    )

    def mix_copy(i, k):
        peer, target = mix_from[i]
        at = pl.ds(k * gather_span, gather_span)
        return rcopy(
            part.at[own_at(target), at],
            mixin.at[i, :, at],
            mix_send.at[i, k],
            mix_recv.at[i, k],
            peer,
        )

    for k in range(GATHER_CHUNKS):
        at = slice(k * gather_span, (k + 1) * gather_span)
        part[:, at] = jnp.dot(attv[...], wov[:, at], preferred_element_type=f32).astype(bf16)
        for i in range(3):
            mix_copy(i, k).start()
    for copy in weight_loads[2]:
        copy.start()

    load_res.wait()
    load_gain.wait()
    spot = lambda c, x, z: pl.ds(
        pl.multiple_of(c * half + x * quarter + z * own, own), own
    )
    mine = spot(core, tx, me)
    gather_at = lambda k: pl.ds(
        k * gather_span, gather_span + (LANES if k == GATHER_CHUNKS - 1 else 0)
    )

    def nz_copy(to, z, k):
        at = nall.at[spot(core, tx, z), gather_at(k)]
        return rcopy(at, at, nz_send.at[to, k], nz_recv.at[z, k], {"sec": to})

    def nx_copy(x, z, k):
        at = nall.at[spot(core, x, z), gather_at(k)]
        return rcopy(at, at, nx_send.at[z, k], nx_recv.at[z, k], x_peer)

    def nc_copy(c, x, k):
        start = pl.multiple_of(c * half + x * quarter, quarter)
        at = nall.at[pl.ds(start, quarter), gather_at(k)]
        return rcopy(at, at, nc_send.at[x, k], nc_recv.at[x, k], c_peer)

    squares = jnp.zeros((own, 1), f32)
    for k in range(GATHER_CHUNKS):
        at = slice(k * gather_span, (k + 1) * gather_span)
        for i in range(3):
            mix_copy(i, k).wait_recv()
        total = part[own_at(rank), at].astype(f32)
        for i in range(3):
            total = total + mixin[i, :, at].astype(f32)
        total = total + resv[:, at].astype(f32)
        stream[:, at] = total
        squares = squares + jnp.sum(total * total, axis=1, keepdims=True)
        nall[mine, at] = (total * gainv[:, at]).astype(bf16)
        if k == GATHER_CHUNKS - 1:
            left = jnp.broadcast_to(lax.rsqrt(squares / width + norm_eps), (own, LANES))
            lane = lax.broadcasted_iota(jnp.int32, (own, LANES), 1)
            parts = jnp.zeros((own, LANES), f32)
            for i in range(3):
                now = left.astype(bf16).astype(f32)
                parts = jnp.where(lane == i, now, parts)
                left = left - now
            nall[mine, width:] = parts.astype(bf16)
        nearest(lambda z, k=k: nz_copy(z, me, k).start())
        nx_copy(tx, me, k).start()

    for d in range(1, n_sec):
        route_copy(d, sec_of(d)).wait_recv()
    facts = routev[0]
    for z in range(1, n_sec):
        facts = facts + routev[z]
    here = E // n_sec
    capacity = n_sec * MOSTB
    first, second = facts[0:1, :], facts[1:2, :]
    code_a, code_b = facts[2:3, :], facts[3:4, :]
    base = (me * here).astype(f32)
    local = lax.broadcasted_iota(jnp.int32, (8, tokens), 0).astype(f32) + base
    member = jnp.where((first == local) | (second == local), 1.0, 0.0)
    before = jnp.where(
        lax.broadcasted_iota(jnp.int32, (tokens, tokens), 0)
        < lax.broadcasted_iota(jnp.int32, (tokens, tokens), 1),
        1.0,
        0.0,
    ).astype(bf16)
    standing = jnp.dot(member.astype(bf16), before, preferred_element_type=f32)
    slot = lax.broadcasted_iota(jnp.int32, (capacity, tokens), 0).astype(f32)
    picks = []
    for e in range(here):
        pick = jnp.where((standing[e : e + 1, :] == slot) & (member[e : e + 1, :] > 0.5), 1.0, 0.0)
        coef = jnp.where(first == base + e, code_a, 0.0) + jnp.where(second == base + e, code_b, 0.0)
        coef = coef / (code_a + code_b)
        share = jnp.sum(pick * coef, axis=1, keepdims=True)
        sharev[e * capacity : (e + 1) * capacity, :] = jnp.broadcast_to(share, (capacity, 128))
        picks.append(pick)
    pick = jnp.concatenate(picks, axis=0)
    pickv[...] = pick.astype(bf16)
    pickt[...] = jnp.transpose(pick).astype(bf16)


    def from_z(k):
        def visit(z):
            nz_copy(z, z, k).wait_recv()
            nx_copy(tx, z, k).start()

        nearest(visit)
        nc_copy(core, tx, k).start()

    def from_x(k):
        for z in range(n_sec):
            nx_copy(1 - tx, z, k).wait_recv()
        nc_copy(core, 1 - tx, k).start()

    def pack(k):
        for x in (tx, 1 - tx):
            nc_copy(1 - core, x, k).wait_recv()
        got = jnp.dot(pickv[...], nall[:, gather_at(k)], preferred_element_type=f32)
        packed[:, : got.shape[1]] = got.astype(bf16)

    units = wgv.shape[1] // here

    def expand(e, k):
        slots = slice(e * capacity, (e + 1) * capacity)
        of = slice(e * units, (e + 1) * units)
        at = slice(k * gather_span, (k + 1) * gather_span)
        x = packed[slots, :gather_span]
        gate = jnp.dot(x, wgv[at, of], preferred_element_type=f32)
        up = jnp.dot(x, wuv[at, of], preferred_element_type=f32)
        if k:
            gate = gate + gacc[slots, :]
            up = up + uacc[slots, :]
        if k < GATHER_CHUNKS - 1:
            gacc[slots, :] = gate
            uacc[slots, :] = up
            return
        scale = jnp.sum(
            packed[slots, gather_span : gather_span + LANES].astype(f32), axis=1, keepdims=True
        )
        gate = gate * scale
        act = gate / (1.0 + jnp.exp(-gate)) * (up * scale)
        hidden[slots, :] = act.astype(bf16)

    arrivals = [functools.partial(from_z, k) for k in range(GATHER_CHUNKS)]
    arrivals += [functools.partial(from_x, k) for k in range(GATHER_CHUNKS)]

    def forward(count):
        for step in arrivals[:count]:
            step()
        del arrivals[:count]

    forward(5)
    for copy in weight_loads[0] + weight_loads[1]:
        copy.wait()
    for k in range(GATHER_CHUNKS):
        pack(k)
        for e in range(here):
            expand(e, k)
            forward(1)

    for k in range(GATHER_CHUNKS):
        nearest(lambda z, k=k: nz_copy(z, me, k).wait_send())
        for z in range(n_sec):
            nx_copy(tx, z, k).wait_send()
        for x in (tx, 1 - tx):
            nc_copy(core, x, k).wait_send()
    for copy in weight_loads[2]:
        copy.wait()
    pout, acc = nall, gacc
    edges = [0]
    for eighths in RETURN_EIGHTHS:
        edges.append(edges[-1] + eighths * width // sum(RETURN_EIGHTHS))
    chunks = len(RETURN_EIGHTHS)
    return_at = lambda c: slice(edges[c], edges[c + 1])
    span_at = lambda c: pl.ds(edges[c], edges[c + 1] - edges[c])

    def shrink(c):
        at = return_at(c)
        outs = []
        for e in range(here):
            slots = slice(e * capacity, (e + 1) * capacity)
            y = jnp.dot(
                hidden[slots, :],
                wdv[e * units : (e + 1) * units, at],
                preferred_element_type=f32,
            )
            outs.append((y * sharev[slots, 0:1]).astype(bf16))
        y = jnp.concatenate(outs, axis=0)
        pout[:, at] = jnp.dot(pickt[...], y, preferred_element_type=f32).astype(bf16)

    half_at = lambda c: pl.ds(pl.multiple_of(c * half, half), half)
    quarter_at = lambda x: pl.ds(pl.multiple_of(x * quarter, quarter), quarter)

    def c1_copy(c):
        at = span_at(c)
        return rcopy(
            pout.at[half_at(1 - core), at], r1.at[:, at], c1_send.at[c], c1_recv.at[c], c_peer
        )

    def x2_copy(c):
        at = span_at(c)
        return rcopy(x_out.at[:, at], r2.at[:, at], x2_send.at[c], x2_recv.at[c], x_peer)

    def z3_copy(c, d, z, device):
        at = span_at(c)
        return rcopy(
            z_out.at[own_at(sec_of(d)), at],
            r3.at[own_at(z), at],
            z3_send.at[c, d],
            z3_recv.at[c, z],
            device,
        )

    def cross_core(c):
        at = return_at(c)
        c1_copy(c).wait_recv()
        other = pl.ds(pl.multiple_of(core * half + (1 - tx) * quarter, quarter), quarter)
        same = pl.ds(pl.multiple_of(core * half + tx * quarter, quarter), quarter)
        x_out[:, at] = (
            pout[other, at].astype(f32) + r1[quarter_at(1 - tx), at].astype(f32)
        ).astype(bf16)
        x2_copy(c).start()
        acc[:quarter, at] = pout[same, at].astype(f32) + r1[quarter_at(tx), at].astype(f32)

    def cross_x(c):
        at = return_at(c)
        x2_copy(c).wait_recv()
        total = acc[:quarter, at] + r2[:, at].astype(f32)
        acc[:quarter, at] = total
        z_out[:, at] = total.astype(bf16)
        for d in range(n_sec - 1, 0, -1):
            z3_copy(c, d, me, {"sec": sec_of(d)}).start()

    def cross_z(c):
        at = return_at(c)
        total = stream[:, at] + acc[own_at(me), at]
        for d in range(1, n_sec):
            z = sec_of(d)
            z3_copy(c, d, z, {"sec": z}).wait_recv()
            total = total + r3[own_at(z), at].astype(f32)
        out[:, at] = total.astype(bf16)

    for c in range(chunks):
        shrink(c)
        c1_copy(c).start()
        if c:
            cross_core(c - 1)
    cross_core(chunks - 1)
    for c in range(chunks):
        cross_x(c)
    for c in range(chunks):
        cross_z(c)

    for which, ref in enumerate((kv, vv)):
        for d in range(1, reach + 1):

            @pl.when(me + d < n_sec)
            def _():
                kv_copy(which, ref, d, me, {"sec": sec_of(d)}).wait_send()

    for d in range(1, n_sec):
        route_copy(d, me).wait_send()
    for i in range(3):
        for k in range(GATHER_CHUNKS):
            mix_copy(i, k).wait_send()
    for c in range(chunks):
        c1_copy(c).wait_send()
        x2_copy(c).wait_send()
        for d in range(1, n_sec):
            z3_copy(c, d, me, {"sec": sec_of(d)}).wait_send()


def fused_device(
    query,
    keys,
    values,
    residual,
    out_weight,
    norm_gain,
    expert_ids,
    gate_codes,
    doc_lengths,
    w_gate,
    w_up,
    w_down,
):
    n_sec = lax.axis_size("sec")
    rows, width = residual.shape
    own = rows // 4
    tokens = n_sec * rows
    here = E // n_sec
    slots = here * n_sec * MOSTB
    kv_width = query.shape[1] * KEY_VALUE_HEADS // QUERY_HEAD_COUNT
    f32, bf16 = jnp.float32, jnp.bfloat16
    V, dma = pltpu.VMEM, pltpu.SemaphoreType.DMA
    anywhere = pl.BlockSpec(memory_space=pl.ANY)
    return pl.pallas_call(
        functools.partial(layer_kernel, n_sec, doc_lengths.shape[0]),
        out_shape=pltpu.VMEM((own, width), bf16),
        in_specs=[pl.BlockSpec(memory_space=pltpu.SMEM)] + [anywhere] * 11,
        out_specs=pl.BlockSpec(memory_space=pltpu.VMEM),
        scratch_shapes=[
            V(query.shape, bf16),
            V((tokens, kv_width), bf16),
            V((tokens, kv_width), bf16),
            V(query.shape, bf16),
            V((own, width), bf16),
            V((1, width), f32),
            V(expert_ids.shape[::-1], jnp.int32),
            V(gate_codes.shape[::-1], jnp.int32),
            V((n_sec, 8, tokens), f32),
            V(w_gate.shape[1:], bf16),
            V(w_up.shape[1:], bf16),
            V(w_down.shape[1:], bf16),
            V((rows, width), bf16),
            V((3, own, width), bf16),
            V((own, width), f32),
            V((tokens, width + LANES), bf16),
            V((slots, width // GATHER_CHUNKS + LANES), bf16),
            V((slots, w_gate.shape[2] // here), f32),
            V((slots, w_gate.shape[2] // here), f32),
            V((slots, w_gate.shape[2] // here), bf16),
            V((slots, tokens), bf16),
            V((tokens, slots), bf16),
            V((slots, LANES), f32),
            V((tokens // 2, width), bf16),
            V((tokens // 4, width), bf16),
            V((tokens // 4, width), bf16),
            V((tokens // 4, width), bf16),
            V((tokens // 4, width), bf16),
            dma((8,)),
            dma((3, WEIGHT_CHUNKS)),
            dma((2, n_sec)),
            dma((2, n_sec)),
            dma((n_sec,)),
            dma((n_sec,)),
            *[dma((3, GATHER_CHUNKS))] * 2,
            *[dma((n_sec, GATHER_CHUNKS))] * 4,
            *[dma((2, GATHER_CHUNKS))] * 2,
            *[dma((len(RETURN_EIGHTHS),))] * 4,
            *[dma((len(RETURN_EIGHTHS), n_sec))] * 2,
        ],
        compiler_params=pltpu.CompilerParams(
            collective_id=0, has_side_effects=True, vmem_limit_bytes=66900000
        ),
    )(
        doc_lengths,
        query,
        keys,
        values,
        residual,
        out_weight,
        norm_gain.reshape(1, width),
        expert_ids.T,
        gate_codes.T,
        w_gate,
        w_up,
        w_down,
    )


def whole_in_vmem(mesh):
    shape = mesh.shape
    return shape["tp"] == 2 and shape["pp"] == 2 and shape["sec"] > 1 and E % shape["sec"] == 0


def solution(mesh):
    in_specs = (
        P(("groups", "sec"), ("tp", "pp")),
        P(("groups", "sec"), "tp"),
        P(("groups", "sec"), "tp"),
        P(("groups", "sec"), None),
        P(("tp", "pp"), None),
        P(),
        P(("groups", "sec"), None),
        P(("groups", "sec"), None),
        P("groups"),
        P(("tp", "pp"), None, "sec"),
        P(("tp", "pp"), None, "sec"),
        P(("tp", "pp"), "sec", None),
    )
    out_specs = P(("groups", "sec", "tp", "pp"), None)
    return jax.shard_map(
        fused_device if whole_in_vmem(mesh) else per_device,
        mesh=mesh,
        in_specs=in_specs,
        out_specs=out_specs,
        check_vma=False,
    )
```

```python
import functools

import jax
import jax.numpy as jnp
from jax import lax
from jax.experimental import pallas as pl
from jax.experimental.pallas import tpu as pltpu
from jax.sharding import PartitionSpec as P

QUERY_HEAD_COUNT = 32
KEY_VALUE_HEADS = 8
HEAD_DIMENSION = 128
E = 8
MOSTB = 32


neg_fill = -1e30
norm_eps = 1e-05


def doc_index(positions, doc_ends):
    return jnp.sum((positions[:, None] >= doc_ends[None, :]).astype(jnp.int32), axis=1)


def running_sum(counts):
    order = jnp.arange(counts.shape[0], dtype=jnp.int32)
    upto = (order[None, :] <= order[:, None]).reshape(order.shape * 2 + (1,) * (counts.ndim - 1))
    return jnp.sum(jnp.where(upto, counts[None], 0), axis=1)


def rms_scale(stream, norm_gain):
    meansq = jnp.mean(stream * stream, axis=1, keepdims=True)
    return (stream * lax.rsqrt(meansq + norm_eps) * norm_gain).astype(jnp.bfloat16)


def per_device(
    query,
    keys,
    values,
    residual,
    out_weight,
    norm_gain,
    expert_ids,
    gate_codes,
    doc_lengths,
    w_gate,
    w_up,
    w_down,
):
    block_rows = query.shape[0]
    head_size = HEAD_DIMENSION
    q_heads = query.shape[1] // head_size
    kv_heads = keys.shape[1] // head_size
    group_width = QUERY_HEAD_COUNT // KEY_VALUE_HEADS
    width = residual.shape[1]
    sec_count = lax.axis_size("sec")
    rank_count = lax.axis_size("tp") * lax.axis_size("pp")
    pp_index = lax.axis_index("pp")
    rank_index = lax.axis_index("tp") * lax.axis_size("pp") + pp_index
    own_rows = block_rows // rank_count
    own_start = rank_index * own_rows
    doc_ends = running_sum(doc_lengths)
    query_pos = lax.axis_index("sec") * block_rows + jnp.arange(block_rows, dtype=jnp.int32)
    query_doc = doc_index(query_pos, doc_ends)
    kv_pick = (pp_index * q_heads + jnp.arange(q_heads, dtype=jnp.int32)) // group_width
    query_heads = query.reshape(block_rows, q_heads, head_size)
    scale = head_size ** (-0.5)
    run_max = jnp.full((q_heads, block_rows), neg_fill, jnp.float32)
    key_piece = lax.all_gather(keys, "sec", axis=0, tiled=True)
    value_piece = lax.all_gather(values, "sec", axis=0, tiled=True)
    count = key_piece.shape[0]
    key_heads = jnp.take(key_piece.reshape(count, kv_heads, head_size), kv_pick, axis=1)
    value_heads = jnp.take(value_piece.reshape(count, kv_heads, head_size), kv_pick, axis=1)
    scores = (
        jnp.einsum("qhd,khd->hqk", query_heads, key_heads, preferred_element_type=jnp.float32)
        * scale
    )
    key_pos = jnp.arange(count, dtype=jnp.int32)
    allowed = (key_pos[None, :] <= query_pos[:, None]) & (
        doc_index(key_pos, doc_ends)[None, :] == query_doc[:, None]
    )
    scores = jnp.where(allowed[None], scores, neg_fill)
    new_max = jnp.maximum(run_max, jnp.max(scores, axis=2))
    probs = jnp.where(allowed[None], jnp.exp(scores - new_max[:, :, None]), 0.0)
    run_total = jnp.sum(probs, axis=2)
    run_acc = jnp.einsum(
        "hqk,khd->hqd", probs.astype(jnp.bfloat16), value_heads, preferred_element_type=jnp.float32
    )
    run_max, run_total, run_acc = (new_max, run_total, run_acc)
    attended = (
        (run_acc / run_total[:, :, None])
        .transpose(1, 0, 2)
        .reshape(block_rows, q_heads * head_size)
        .astype(jnp.bfloat16)
    )
    rows_in = attended
    mixed_own = lax.psum_scatter(
        jnp.dot(rows_in, out_weight, preferred_element_type=jnp.float32).astype(jnp.bfloat16),
        ("tp", "pp"),
        scatter_dimension=0,
        tiled=True,
    ).astype(jnp.float32)
    stream_own = (
        lax.dynamic_slice_in_dim(residual, own_start, own_rows, 0).astype(jnp.float32) + mixed_own
    )
    normed = lax.all_gather(rms_scale(stream_own, norm_gain), ("tp", "pp"), axis=0, tiled=True)
    capacity = MOSTB
    experts_here = max(1, E // sec_count)
    halves = max(1, sec_count // E)
    route_hits = (expert_ids[:, :, None] == jnp.arange(E, dtype=jnp.int32)[None, None, :]).astype(
        jnp.int32
    )
    member = jnp.sum(route_hits, axis=1)
    slots = running_sum(member) - 1
    slot_pick = jnp.sum(route_hits * slots[:, None, :], axis=2)
    codes = gate_codes.astype(jnp.float32)
    shares = codes / jnp.sum(codes, axis=1, keepdims=True)
    slot_range = jnp.arange(capacity, dtype=jnp.int32)
    select = (
        (slots.T[:, None, :] == slot_range[None, :, None]) & (member.T[:, None, :] == 1)
    ).astype(jnp.bfloat16)
    gate_local = w_gate[0].reshape(width, experts_here, -1)
    up_local = w_up[0].reshape(width, experts_here, -1)
    down_local = w_down[0].reshape(experts_here, -1, width)
    packed = jnp.einsum("ecr,rd->ecd", select, normed, preferred_element_type=jnp.float32).astype(
        jnp.bfloat16
    )
    packed = jnp.repeat(packed, halves, axis=0)
    rows_in = lax.all_to_all(
        packed.reshape(sec_count, experts_here, capacity, normed.shape[1]),
        "sec",
        split_axis=0,
        concat_axis=0,
        tiled=True,
    )
    gate = jnp.einsum("sxmd,dxf->sxmf", rows_in, gate_local, preferred_element_type=jnp.float32)
    up = jnp.einsum("sxmd,dxf->sxmf", rows_in, up_local, preferred_element_type=jnp.float32)
    hidden = (jax.nn.silu(gate) * up).astype(jnp.bfloat16)
    partial_out = jnp.einsum(
        "sxmf,xfd->sxmd", hidden, down_local, preferred_element_type=jnp.float32
    )
    returned = lax.all_to_all(
        partial_out.astype(jnp.bfloat16), "sec", split_axis=0, concat_axis=0, tiled=True
    ).astype(partial_out.dtype)
    flat_parts = returned.reshape(sec_count * experts_here * capacity, width)
    half_range = jnp.arange(halves, dtype=jnp.int32)
    top_count = expert_ids.shape[1]
    index = ((expert_ids * halves)[:, :, None] + half_range[None, None, :]) * capacity + slot_pick[
        :, :, None
    ]
    picked = jnp.take(flat_parts, index.reshape(-1), axis=0).reshape(
        own_rows * lax.axis_size(("tp", "pp")), top_count, halves, width
    )
    mixture_own = lax.psum_scatter(
        jnp.sum(picked * shares[:, :, None, None], axis=(1, 2)).astype(jnp.bfloat16),
        ("tp", "pp"),
        scatter_dimension=0,
        tiled=True,
    ).astype(jnp.float32)
    return (stream_own + mixture_own).astype(jnp.bfloat16)


MESH = pl.DeviceIdType.MESH
LANES = 128
GATHER_CHUNKS = 4
RETURN_EIGHTHS = (2, 2, 2, 2)
WEIGHT_CHUNKS = 4


def rcopy(src, dst, send_sem, recv_sem, device):
    return pltpu.make_async_remote_copy(
        src_ref=src,
        dst_ref=dst,
        send_sem=send_sem,
        recv_sem=recv_sem,
        device_id=device,
        device_id_type=MESH,
    )


def layer_kernel(
    n_sec,
    docs,
    lengths,
    query,
    keys,
    values,
    residual,
    out_weight,
    norm_gain,
    ids,
    codes,
    w_gate,
    w_up,
    w_down,
    out,
    qv,
    kv,
    vv,
    attv,
    resv,
    gainv,
    idsv,
    codesv,
    routev,
    wgv,
    wuv,
    wdv,
    part,
    mixin,
    stream,
    nall,
    packed,
    gacc,
    uacc,
    hidden,
    pickv,
    pickt,
    sharev,
    r1,
    x_out,
    r2,
    z_out,
    r3,
    load_sem,
    w_sem,
    kv_send,
    kv_recv,
    route_send,
    route_recv,
    mix_send,
    mix_recv,
    nz_send,
    nz_recv,
    nx_send,
    nx_recv,
    nc_send,
    nc_recv,
    c1_send,
    c1_recv,
    x2_send,
    x2_recv,
    z3_send,
    z3_recv,
):
    f32, bf16 = jnp.float32, jnp.bfloat16
    me, tx, core = lax.axis_index("sec"), lax.axis_index("tp"), lax.axis_index("pp")
    rank = tx * 2 + core
    rows, width = residual.shape
    own = rows // 4
    kv_width = kv.shape[1]
    tokens = n_sec * rows
    half, quarter = tokens // 2, tokens // 4
    x_peer, c_peer = {"tp": 1 - tx}, {"pp": 1 - core}
    d_peer = {"tp": 1 - tx, "pp": 1 - core}
    sec_of = lambda d: lax.rem(me + d, n_sec)
    longest = tokens // 2
    reach = min(n_sec - 1, pl.cdiv(longest - 1, rows))

    near = []
    for i in range(n_sec - 1):
        z = jnp.int32(0)
        for m in range(n_sec):
            order = sorted(set(range(n_sec)) - {m}, key=lambda to: (abs(to - m), -to))
            z = jnp.where(me == m, order[i], z)
        near.append(z)

    def nearest(visit):
        for z in near:
            visit(z)

    def load(src, dst, i):
        copy = pltpu.make_async_copy(src, dst, load_sem.at[i])
        copy.start()
        return copy

    barrier = pltpu.get_barrier_semaphore()
    for d in range(1, n_sec):
        pl.semaphore_signal(barrier, inc=1, device_id={"sec": sec_of(d)}, device_id_type=MESH)
    for peer in (x_peer, c_peer, d_peer):
        pl.semaphore_signal(barrier, inc=1, device_id=peer, device_id_type=MESH)

    columns = pl.ds(pl.multiple_of(core * kv_width, 128), kv_width)
    block = lambda z: pl.ds(pl.multiple_of(z * rows, rows), rows)
    load_k = load(keys.at[:, columns], kv.at[block(me), :], 0)
    load_v = load(values.at[:, columns], vv.at[block(me), :], 1)
    load_ids = load(ids, idsv, 2)
    load_codes = load(codes, codesv, 7)
    load_q = load(query, qv, 3)
    wov = wdv.at[pl.ds(0, out_weight.shape[0]), :]
    load_wo = load(out_weight, wov, 4)
    load_res = load(residual.at[pl.ds(pl.multiple_of(rank * own, own), own), :], resv, 5)
    load_gain = load(norm_gain, gainv, 6)
    weight_loads = []
    for which, (src, dst) in enumerate(((w_gate, wgv), (w_up, wuv), (w_down, wdv))):
        span = dst.shape[1] // WEIGHT_CHUNKS
        loads = []
        for i in range(WEIGHT_CHUNKS):
            piece = pl.ds(i * span, span)
            copy = pltpu.make_async_copy(
                src.at[0, :, piece], dst.at[:, piece], w_sem.at[which, i]
            )
            loads.append(copy)
        weight_loads.append(loads)

    for z in range(n_sec):

        @pl.when((z > me) | (z < me - reach))
        def _():
            kv[z * rows : (z + 1) * rows, :] = jnp.zeros((rows, kv_width), bf16)
            vv[z * rows : (z + 1) * rows, :] = jnp.zeros((rows, kv_width), bf16)

    load_k.wait()
    load_v.wait()
    pl.semaphore_wait(barrier, n_sec + 2)

    def kv_copy(which, ref, d, z, device):
        return rcopy(
            ref.at[block(z), :],
            ref.at[block(z), :],
            kv_send.at[which, d],
            kv_recv.at[which, z],
            device,
        )

    for which, ref in enumerate((kv, vv)):
        for d in range(1, reach + 1):

            @pl.when(me + d < n_sec)
            def _():
                kv_copy(which, ref, d, me, {"sec": sec_of(d)}).start()

    load_ids.wait()
    load_codes.wait()
    given = jnp.concatenate(
        [idsv[...].astype(f32), codesv[...].astype(f32), jnp.zeros((4, rows), f32)], axis=0
    )
    lane = lax.broadcasted_iota(jnp.int32, (rows, tokens), 1)
    row_of = (
        lax.rem(lane // quarter, 2) * (2 * own) + lane // half * own + lax.rem(lane, own)
    )
    here_z = lax.rem(lane, quarter) // own == me
    spread = jnp.where(
        here_z & (row_of == lax.broadcasted_iota(jnp.int32, (rows, tokens), 0)), 1.0, 0.0
    )
    routev[me] = jnp.dot(given.astype(bf16), spread.astype(bf16), preferred_element_type=f32)

    def route_copy(d, z):
        return rcopy(
            routev.at[z], routev.at[z], route_send.at[d], route_recv.at[z], {"sec": sec_of(d)}
        )

    for d in range(1, n_sec):
        route_copy(d, me).start()

    for i in range(WEIGHT_CHUNKS):
        weight_loads[0][i].start()
        weight_loads[1][i].start()

    load_q.wait()
    shape = (rows, tokens)
    query_pos = lax.broadcasted_iota(jnp.int32, shape, 0) + me * rows
    key_pos = lax.broadcasted_iota(jnp.int32, shape, 1)
    query_doc = jnp.zeros(shape, jnp.int32)
    key_doc = jnp.zeros(shape, jnp.int32)
    end = jnp.int32(0)
    for i in range(docs):
        end = end + lengths[i]
        query_doc += (query_pos >= end).astype(jnp.int32)
        key_doc += (key_pos >= end).astype(jnp.int32)
    allowed = jnp.where((key_pos <= query_pos) & (query_doc == key_doc), 1.0, 0.0)
    size = HEAD_DIMENSION
    group_width = QUERY_HEAD_COUNT // KEY_VALUE_HEADS
    allowed = jnp.concatenate([allowed] * group_width, axis=0) > 0.5

    for z in range(n_sec - 1):

        @pl.when((z < me) & (z >= me - reach))
        def _():
            kv_copy(0, kv, 1, z, {"sec": sec_of(1)}).wait_recv()
            kv_copy(1, vv, 1, z, {"sec": sec_of(1)}).wait_recv()

    for g in range(kv_width // size):
        heads = range(g * group_width, (g + 1) * group_width)
        q = jnp.concatenate([qv[:, h * size : (h + 1) * size] for h in heads], axis=0)
        k = kv[:, g * size : (g + 1) * size]
        v = vv[:, g * size : (g + 1) * size]
        scores = lax.dot_general(
            q, k, (((1,), (1,)), ((), ())), preferred_element_type=f32
        ) * (size ** (-0.5))
        scores = jnp.where(allowed, scores, neg_fill)
        top = jnp.max(scores, axis=1, keepdims=True)
        probs = jnp.where(allowed, jnp.exp(scores - top), 0.0)
        total = jnp.sum(probs, axis=1, keepdims=True)
        mixed = jnp.dot(probs.astype(bf16), v, preferred_element_type=f32) / total
        mixed = mixed.astype(bf16)
        for i, h in enumerate(heads):
            attv[:, h * size : (h + 1) * size] = mixed[i * rows : (i + 1) * rows, :]

    load_wo.wait()
    gather_span = width // GATHER_CHUNKS
    own_at = lambda r: pl.ds(pl.multiple_of(r * own, own), own)
    mix_from = (
        (d_peer, (1 - tx) * 2 + 1 - core),
        (x_peer, (1 - tx) * 2 + core),
        (c_peer, tx * 2 + 1 - core),
    )

    def mix_copy(i, k):
        peer, target = mix_from[i]
        at = pl.ds(k * gather_span, gather_span)
        return rcopy(
            part.at[own_at(target), at],
            mixin.at[i, :, at],
            mix_send.at[i, k],
            mix_recv.at[i, k],
            peer,
        )

    for k in range(GATHER_CHUNKS):
        at = slice(k * gather_span, (k + 1) * gather_span)
        part[:, at] = jnp.dot(attv[...], wov[:, at], preferred_element_type=f32).astype(bf16)
        for i in range(3):
            mix_copy(i, k).start()
    for copy in weight_loads[2]:
        copy.start()

    load_res.wait()
    load_gain.wait()
    spot = lambda c, x, z: pl.ds(
        pl.multiple_of(c * half + x * quarter + z * own, own), own
    )
    mine = spot(core, tx, me)
    gather_at = lambda k: pl.ds(
        k * gather_span, gather_span + (LANES if k == GATHER_CHUNKS - 1 else 0)
    )

    def nz_copy(to, z, k):
        at = nall.at[spot(core, tx, z), gather_at(k)]
        return rcopy(at, at, nz_send.at[to, k], nz_recv.at[z, k], {"sec": to})

    def nx_copy(x, z, k):
        at = nall.at[spot(core, x, z), gather_at(k)]
        return rcopy(at, at, nx_send.at[z, k], nx_recv.at[z, k], x_peer)

    def nc_copy(c, x, k):
        start = pl.multiple_of(c * half + x * quarter, quarter)
        at = nall.at[pl.ds(start, quarter), gather_at(k)]
        return rcopy(at, at, nc_send.at[x, k], nc_recv.at[x, k], c_peer)

    squares = jnp.zeros((own, 1), f32)
    for k in range(GATHER_CHUNKS):
        at = slice(k * gather_span, (k + 1) * gather_span)
        for i in range(3):
            mix_copy(i, k).wait_recv()
        total = part[own_at(rank), at].astype(f32)
        for i in range(3):
            total = total + mixin[i, :, at].astype(f32)
        total = total + resv[:, at].astype(f32)
        stream[:, at] = total
        squares = squares + jnp.sum(total * total, axis=1, keepdims=True)
        nall[mine, at] = (total * gainv[:, at]).astype(bf16)
        if k == GATHER_CHUNKS - 1:
            left = jnp.broadcast_to(lax.rsqrt(squares / width + norm_eps), (own, LANES))
            lane = lax.broadcasted_iota(jnp.int32, (own, LANES), 1)
            parts = jnp.zeros((own, LANES), f32)
            for i in range(3):
                now = left.astype(bf16).astype(f32)
                parts = jnp.where(lane == i, now, parts)
                left = left - now
            nall[mine, width:] = parts.astype(bf16)
        for z in near[::-1]:
            nz_copy(z, me, k).start()
        nx_copy(tx, me, k).start()

    for d in range(1, n_sec):
        route_copy(d, sec_of(d)).wait_recv()
    facts = routev[0]
    for z in range(1, n_sec):
        facts = facts + routev[z]
    here = E // n_sec
    capacity = n_sec * MOSTB
    first, second = facts[0:1, :], facts[1:2, :]
    code_a, code_b = facts[2:3, :], facts[3:4, :]
    base = (me * here).astype(f32)
    local = lax.broadcasted_iota(jnp.int32, (8, tokens), 0).astype(f32) + base
    member = jnp.where((first == local) | (second == local), 1.0, 0.0)
    before = jnp.where(
        lax.broadcasted_iota(jnp.int32, (tokens, tokens), 0)
        < lax.broadcasted_iota(jnp.int32, (tokens, tokens), 1),
        1.0,
        0.0,
    ).astype(bf16)
    standing = jnp.dot(member.astype(bf16), before, preferred_element_type=f32)
    slot = lax.broadcasted_iota(jnp.int32, (capacity, tokens), 0).astype(f32)
    picks = []
    for e in range(here):
        pick = jnp.where((standing[e : e + 1, :] == slot) & (member[e : e + 1, :] > 0.5), 1.0, 0.0)
        coef = jnp.where(first == base + e, code_a, 0.0) + jnp.where(second == base + e, code_b, 0.0)
        coef = coef / (code_a + code_b)
        share = jnp.sum(pick * coef, axis=1, keepdims=True)
        sharev[e * capacity : (e + 1) * capacity, :] = jnp.broadcast_to(share, (capacity, 128))
        picks.append(pick)
    pick = jnp.concatenate(picks, axis=0)
    pickv[...] = pick.astype(bf16)
    pickt[...] = jnp.transpose(pick).astype(bf16)


    def from_z(k):
        def visit(z):
            nz_copy(z, z, k).wait_recv()
            nx_copy(tx, z, k).start()

        for z in near[::-1]:
            visit(z)
        nc_copy(core, tx, k).start()

    def from_x(k):
        for z in range(n_sec):
            nx_copy(1 - tx, z, k).wait_recv()
        nc_copy(core, 1 - tx, k).start()

    def pack(k):
        for x in (tx, 1 - tx):
            nc_copy(1 - core, x, k).wait_recv()
        got = jnp.dot(pickv[...], nall[:, gather_at(k)], preferred_element_type=f32)
        packed[:, : got.shape[1]] = got.astype(bf16)

    units = wgv.shape[1] // here

    def expand(e, k):
        slots = slice(e * capacity, (e + 1) * capacity)
        of = slice(e * units, (e + 1) * units)
        at = slice(k * gather_span, (k + 1) * gather_span)
        x = packed[slots, :gather_span]
        gate = jnp.dot(x, wgv[at, of], preferred_element_type=f32)
        up = jnp.dot(x, wuv[at, of], preferred_element_type=f32)
        if k:
            gate = gate + gacc[slots, :]
            up = up + uacc[slots, :]
        if k < GATHER_CHUNKS - 1:
            gacc[slots, :] = gate
            uacc[slots, :] = up
            return
        scale = jnp.sum(
            packed[slots, gather_span : gather_span + LANES].astype(f32), axis=1, keepdims=True
        )
        gate = gate * scale
        act = gate / (1.0 + jnp.exp(-gate)) * (up * scale)
        hidden[slots, :] = act.astype(bf16)

    arrivals = [functools.partial(from_z, k) for k in range(GATHER_CHUNKS)]
    arrivals += [functools.partial(from_x, k) for k in range(GATHER_CHUNKS)]

    def forward(count):
        for step in arrivals[:count]:
            step()
        del arrivals[:count]

    forward(6)
    for copy in weight_loads[0] + weight_loads[1]:
        copy.wait()
    for k in range(GATHER_CHUNKS):
        pack(k)
        for e in range(here):
            expand(e, k)
            forward(1)

    for k in range(GATHER_CHUNKS):
        nearest(lambda z, k=k: nz_copy(z, me, k).wait_send())
        for z in range(n_sec):
            nx_copy(tx, z, k).wait_send()
        for x in (tx, 1 - tx):
            nc_copy(core, x, k).wait_send()
    for copy in weight_loads[2]:
        copy.wait()
    pout, acc = nall, gacc
    edges = [0]
    for eighths in RETURN_EIGHTHS:
        edges.append(edges[-1] + eighths * width // sum(RETURN_EIGHTHS))
    chunks = len(RETURN_EIGHTHS)
    return_at = lambda c: slice(edges[c], edges[c + 1])
    span_at = lambda c: pl.ds(edges[c], edges[c + 1] - edges[c])

    def shrink(c):
        at = return_at(c)
        outs = []
        for e in range(here):
            slots = slice(e * capacity, (e + 1) * capacity)
            y = jnp.dot(
                hidden[slots, :],
                wdv[e * units : (e + 1) * units, at],
                preferred_element_type=f32,
            )
            outs.append((y * sharev[slots, 0:1]).astype(bf16))
        y = jnp.concatenate(outs, axis=0)
        pout[:, at] = jnp.dot(pickt[...], y, preferred_element_type=f32).astype(bf16)

    half_at = lambda c: pl.ds(pl.multiple_of(c * half, half), half)
    quarter_at = lambda x: pl.ds(pl.multiple_of(x * quarter, quarter), quarter)

    def c1_copy(c):
        at = span_at(c)
        return rcopy(
            pout.at[half_at(1 - core), at], r1.at[:, at], c1_send.at[c], c1_recv.at[c], c_peer
        )

    def x2_copy(c):
        at = span_at(c)
        return rcopy(x_out.at[:, at], r2.at[:, at], x2_send.at[c], x2_recv.at[c], x_peer)

    def z3_copy(c, d, z, device):
        at = span_at(c)
        return rcopy(
            z_out.at[own_at(sec_of(d)), at],
            r3.at[own_at(z), at],
            z3_send.at[c, d],
            z3_recv.at[c, z],
            device,
        )

    def cross_core(c):
        at = return_at(c)
        c1_copy(c).wait_recv()
        other = pl.ds(pl.multiple_of(core * half + (1 - tx) * quarter, quarter), quarter)
        same = pl.ds(pl.multiple_of(core * half + tx * quarter, quarter), quarter)
        x_out[:, at] = (
            pout[other, at].astype(f32) + r1[quarter_at(1 - tx), at].astype(f32)
        ).astype(bf16)
        x2_copy(c).start()
        acc[:quarter, at] = pout[same, at].astype(f32) + r1[quarter_at(tx), at].astype(f32)

    def cross_x(c):
        at = return_at(c)
        x2_copy(c).wait_recv()
        total = acc[:quarter, at] + r2[:, at].astype(f32)
        acc[:quarter, at] = total
        z_out[:, at] = total.astype(bf16)
        for d in range(n_sec - 1, 0, -1):
            z3_copy(c, d, me, {"sec": sec_of(d)}).start()

    def cross_z(c):
        at = return_at(c)
        total = stream[:, at] + acc[own_at(me), at]
        for d in range(1, n_sec):
            z = sec_of(d)
            z3_copy(c, d, z, {"sec": z}).wait_recv()
            total = total + r3[own_at(z), at].astype(f32)
        out[:, at] = total.astype(bf16)

    for c in range(chunks):
        shrink(c)
        c1_copy(c).start()
        if c:
            cross_core(c - 1)
    cross_core(chunks - 1)
    for c in range(chunks):
        cross_x(c)
    for c in range(chunks):
        cross_z(c)

    for which, ref in enumerate((kv, vv)):
        for d in range(1, reach + 1):

            @pl.when(me + d < n_sec)
            def _():
                kv_copy(which, ref, d, me, {"sec": sec_of(d)}).wait_send()

    for d in range(1, n_sec):
        route_copy(d, me).wait_send()
    for i in range(3):
        for k in range(GATHER_CHUNKS):
            mix_copy(i, k).wait_send()
    for c in range(chunks):
        c1_copy(c).wait_send()
        x2_copy(c).wait_send()
        for d in range(1, n_sec):
            z3_copy(c, d, me, {"sec": sec_of(d)}).wait_send()


def fused_device(
    query,
    keys,
    values,
    residual,
    out_weight,
    norm_gain,
    expert_ids,
    gate_codes,
    doc_lengths,
    w_gate,
    w_up,
    w_down,
):
    n_sec = lax.axis_size("sec")
    rows, width = residual.shape
    own = rows // 4
    tokens = n_sec * rows
    here = E // n_sec
    slots = here * n_sec * MOSTB
    kv_width = query.shape[1] * KEY_VALUE_HEADS // QUERY_HEAD_COUNT
    f32, bf16 = jnp.float32, jnp.bfloat16
    V, dma = pltpu.VMEM, pltpu.SemaphoreType.DMA
    anywhere = pl.BlockSpec(memory_space=pl.ANY)
    return pl.pallas_call(
        functools.partial(layer_kernel, n_sec, doc_lengths.shape[0]),
        out_shape=pltpu.VMEM((own, width), bf16),
        in_specs=[pl.BlockSpec(memory_space=pltpu.SMEM)] + [anywhere] * 11,
        out_specs=pl.BlockSpec(memory_space=pltpu.VMEM),
        scratch_shapes=[
            V(query.shape, bf16),
            V((tokens, kv_width), bf16),
            V((tokens, kv_width), bf16),
            V(query.shape, bf16),
            V((own, width), bf16),
            V((1, width), f32),
            V(expert_ids.shape[::-1], jnp.int32),
            V(gate_codes.shape[::-1], jnp.int32),
            V((n_sec, 8, tokens), f32),
            V(w_gate.shape[1:], bf16),
            V(w_up.shape[1:], bf16),
            V(w_down.shape[1:], bf16),
            V((rows, width), bf16),
            V((3, own, width), bf16),
            V((own, width), f32),
            V((tokens, width + LANES), bf16),
            V((slots, width // GATHER_CHUNKS + LANES), bf16),
            V((slots, w_gate.shape[2] // here), f32),
            V((slots, w_gate.shape[2] // here), f32),
            V((slots, w_gate.shape[2] // here), bf16),
            V((slots, tokens), bf16),
            V((tokens, slots), bf16),
            V((slots, LANES), f32),
            V((tokens // 2, width), bf16),
            V((tokens // 4, width), bf16),
            V((tokens // 4, width), bf16),
            V((tokens // 4, width), bf16),
            V((tokens // 4, width), bf16),
            dma((8,)),
            dma((3, WEIGHT_CHUNKS)),
            dma((2, n_sec)),
            dma((2, n_sec)),
            dma((n_sec,)),
            dma((n_sec,)),
            *[dma((3, GATHER_CHUNKS))] * 2,
            *[dma((n_sec, GATHER_CHUNKS))] * 4,
            *[dma((2, GATHER_CHUNKS))] * 2,
            *[dma((len(RETURN_EIGHTHS),))] * 4,
            *[dma((len(RETURN_EIGHTHS), n_sec))] * 2,
        ],
        compiler_params=pltpu.CompilerParams(
            collective_id=0, has_side_effects=True, vmem_limit_bytes=66900000
        ),
    )(
        doc_lengths,
        query,
        keys,
        values,
        residual,
        out_weight,
        norm_gain.reshape(1, width),
        expert_ids.T,
        gate_codes.T,
        w_gate,
        w_up,
        w_down,
    )


def whole_in_vmem(mesh):
    shape = mesh.shape
    return shape["tp"] == 2 and shape["pp"] == 2 and shape["sec"] > 1 and E % shape["sec"] == 0


def solution(mesh):
    in_specs = (
        P(("groups", "sec"), ("tp", "pp")),
        P(("groups", "sec"), "tp"),
        P(("groups", "sec"), "tp"),
        P(("groups", "sec"), None),
        P(("tp", "pp"), None),
        P(),
        P(("groups", "sec"), None),
        P(("groups", "sec"), None),
        P("groups"),
        P(("tp", "pp"), None, "sec"),
        P(("tp", "pp"), None, "sec"),
        P(("tp", "pp"), "sec", None),
    )
    out_specs = P(("groups", "sec", "tp", "pp"), None)
    return jax.shard_map(
        fused_device if whole_in_vmem(mesh) else per_device,
        mesh=mesh,
        in_specs=in_specs,
        out_specs=out_specs,
        check_vma=False,
    )
```

```python
import functools

import jax
import jax.numpy as jnp
from jax import lax
from jax.experimental import pallas as pl
from jax.experimental.pallas import tpu as pltpu
from jax.sharding import PartitionSpec as P

QUERY_HEAD_COUNT = 32
KEY_VALUE_HEADS = 8
HEAD_DIMENSION = 128
E = 8
MOSTB = 32


neg_fill = -1e30
norm_eps = 1e-05


def doc_index(positions, doc_ends):
    return jnp.sum((positions[:, None] >= doc_ends[None, :]).astype(jnp.int32), axis=1)


def running_sum(counts):
    order = jnp.arange(counts.shape[0], dtype=jnp.int32)
    upto = (order[None, :] <= order[:, None]).reshape(order.shape * 2 + (1,) * (counts.ndim - 1))
    return jnp.sum(jnp.where(upto, counts[None], 0), axis=1)


def rms_scale(stream, norm_gain):
    meansq = jnp.mean(stream * stream, axis=1, keepdims=True)
    return (stream * lax.rsqrt(meansq + norm_eps) * norm_gain).astype(jnp.bfloat16)


def per_device(
    query,
    keys,
    values,
    residual,
    out_weight,
    norm_gain,
    expert_ids,
    gate_codes,
    doc_lengths,
    w_gate,
    w_up,
    w_down,
):
    block_rows = query.shape[0]
    head_size = HEAD_DIMENSION
    q_heads = query.shape[1] // head_size
    kv_heads = keys.shape[1] // head_size
    group_width = QUERY_HEAD_COUNT // KEY_VALUE_HEADS
    width = residual.shape[1]
    sec_count = lax.axis_size("sec")
    rank_count = lax.axis_size("tp") * lax.axis_size("pp")
    pp_index = lax.axis_index("pp")
    rank_index = lax.axis_index("tp") * lax.axis_size("pp") + pp_index
    own_rows = block_rows // rank_count
    own_start = rank_index * own_rows
    doc_ends = running_sum(doc_lengths)
    query_pos = lax.axis_index("sec") * block_rows + jnp.arange(block_rows, dtype=jnp.int32)
    query_doc = doc_index(query_pos, doc_ends)
    kv_pick = (pp_index * q_heads + jnp.arange(q_heads, dtype=jnp.int32)) // group_width
    query_heads = query.reshape(block_rows, q_heads, head_size)
    scale = head_size ** (-0.5)
    run_max = jnp.full((q_heads, block_rows), neg_fill, jnp.float32)
    key_piece = lax.all_gather(keys, "sec", axis=0, tiled=True)
    value_piece = lax.all_gather(values, "sec", axis=0, tiled=True)
    count = key_piece.shape[0]
    key_heads = jnp.take(key_piece.reshape(count, kv_heads, head_size), kv_pick, axis=1)
    value_heads = jnp.take(value_piece.reshape(count, kv_heads, head_size), kv_pick, axis=1)
    scores = (
        jnp.einsum("qhd,khd->hqk", query_heads, key_heads, preferred_element_type=jnp.float32)
        * scale
    )
    key_pos = jnp.arange(count, dtype=jnp.int32)
    allowed = (key_pos[None, :] <= query_pos[:, None]) & (
        doc_index(key_pos, doc_ends)[None, :] == query_doc[:, None]
    )
    scores = jnp.where(allowed[None], scores, neg_fill)
    new_max = jnp.maximum(run_max, jnp.max(scores, axis=2))
    probs = jnp.where(allowed[None], jnp.exp(scores - new_max[:, :, None]), 0.0)
    run_total = jnp.sum(probs, axis=2)
    run_acc = jnp.einsum(
        "hqk,khd->hqd", probs.astype(jnp.bfloat16), value_heads, preferred_element_type=jnp.float32
    )
    run_max, run_total, run_acc = (new_max, run_total, run_acc)
    attended = (
        (run_acc / run_total[:, :, None])
        .transpose(1, 0, 2)
        .reshape(block_rows, q_heads * head_size)
        .astype(jnp.bfloat16)
    )
    rows_in = attended
    mixed_own = lax.psum_scatter(
        jnp.dot(rows_in, out_weight, preferred_element_type=jnp.float32).astype(jnp.bfloat16),
        ("tp", "pp"),
        scatter_dimension=0,
        tiled=True,
    ).astype(jnp.float32)
    stream_own = (
        lax.dynamic_slice_in_dim(residual, own_start, own_rows, 0).astype(jnp.float32) + mixed_own
    )
    normed = lax.all_gather(rms_scale(stream_own, norm_gain), ("tp", "pp"), axis=0, tiled=True)
    capacity = MOSTB
    experts_here = max(1, E // sec_count)
    halves = max(1, sec_count // E)
    route_hits = (expert_ids[:, :, None] == jnp.arange(E, dtype=jnp.int32)[None, None, :]).astype(
        jnp.int32
    )
    member = jnp.sum(route_hits, axis=1)
    slots = running_sum(member) - 1
    slot_pick = jnp.sum(route_hits * slots[:, None, :], axis=2)
    codes = gate_codes.astype(jnp.float32)
    shares = codes / jnp.sum(codes, axis=1, keepdims=True)
    slot_range = jnp.arange(capacity, dtype=jnp.int32)
    select = (
        (slots.T[:, None, :] == slot_range[None, :, None]) & (member.T[:, None, :] == 1)
    ).astype(jnp.bfloat16)
    gate_local = w_gate[0].reshape(width, experts_here, -1)
    up_local = w_up[0].reshape(width, experts_here, -1)
    down_local = w_down[0].reshape(experts_here, -1, width)
    packed = jnp.einsum("ecr,rd->ecd", select, normed, preferred_element_type=jnp.float32).astype(
        jnp.bfloat16
    )
    packed = jnp.repeat(packed, halves, axis=0)
    rows_in = lax.all_to_all(
        packed.reshape(sec_count, experts_here, capacity, normed.shape[1]),
        "sec",
        split_axis=0,
        concat_axis=0,
        tiled=True,
    )
    gate = jnp.einsum("sxmd,dxf->sxmf", rows_in, gate_local, preferred_element_type=jnp.float32)
    up = jnp.einsum("sxmd,dxf->sxmf", rows_in, up_local, preferred_element_type=jnp.float32)
    hidden = (jax.nn.silu(gate) * up).astype(jnp.bfloat16)
    partial_out = jnp.einsum(
        "sxmf,xfd->sxmd", hidden, down_local, preferred_element_type=jnp.float32
    )
    returned = lax.all_to_all(
        partial_out.astype(jnp.bfloat16), "sec", split_axis=0, concat_axis=0, tiled=True
    ).astype(partial_out.dtype)
    flat_parts = returned.reshape(sec_count * experts_here * capacity, width)
    half_range = jnp.arange(halves, dtype=jnp.int32)
    top_count = expert_ids.shape[1]
    index = ((expert_ids * halves)[:, :, None] + half_range[None, None, :]) * capacity + slot_pick[
        :, :, None
    ]
    picked = jnp.take(flat_parts, index.reshape(-1), axis=0).reshape(
        own_rows * lax.axis_size(("tp", "pp")), top_count, halves, width
    )
    mixture_own = lax.psum_scatter(
        jnp.sum(picked * shares[:, :, None, None], axis=(1, 2)).astype(jnp.bfloat16),
        ("tp", "pp"),
        scatter_dimension=0,
        tiled=True,
    ).astype(jnp.float32)
    return (stream_own + mixture_own).astype(jnp.bfloat16)


MESH = pl.DeviceIdType.MESH
LANES = 128
GATHER_CHUNKS = 4
RETURN_EIGHTHS = (2, 2, 2, 2)
WEIGHT_CHUNKS = 4


def rcopy(src, dst, send_sem, recv_sem, device):
    return pltpu.make_async_remote_copy(
        src_ref=src,
        dst_ref=dst,
        send_sem=send_sem,
        recv_sem=recv_sem,
        device_id=device,
        device_id_type=MESH,
    )


def layer_kernel(
    n_sec,
    docs,
    lengths,
    query,
    keys,
    values,
    residual,
    out_weight,
    norm_gain,
    ids,
    codes,
    w_gate,
    w_up,
    w_down,
    out,
    qv,
    kv,
    vv,
    attv,
    resv,
    gainv,
    idsv,
    codesv,
    routev,
    wgv,
    wuv,
    wdv,
    part,
    mixin,
    stream,
    nall,
    packed,
    gacc,
    uacc,
    hidden,
    pickv,
    pickt,
    sharev,
    r1,
    x_out,
    r2,
    z_out,
    r3,
    load_sem,
    w_sem,
    kv_send,
    kv_recv,
    route_send,
    route_recv,
    mix_send,
    mix_recv,
    nz_send,
    nz_recv,
    nx_send,
    nx_recv,
    nc_send,
    nc_recv,
    c1_send,
    c1_recv,
    x2_send,
    x2_recv,
    z3_send,
    z3_recv,
):
    f32, bf16 = jnp.float32, jnp.bfloat16
    me, tx, core = lax.axis_index("sec"), lax.axis_index("tp"), lax.axis_index("pp")
    rank = tx * 2 + core
    rows, width = residual.shape
    own = rows // 4
    kv_width = kv.shape[1]
    tokens = n_sec * rows
    half, quarter = tokens // 2, tokens // 4
    x_peer, c_peer = {"tp": 1 - tx}, {"pp": 1 - core}
    d_peer = {"tp": 1 - tx, "pp": 1 - core}
    sec_of = lambda d: lax.rem(me + d, n_sec)
    longest = tokens // 2
    reach = min(n_sec - 1, pl.cdiv(longest - 1, rows))

    near = []
    for i in range(n_sec - 1):
        z = jnp.int32(0)
        for m in range(n_sec):
            order = sorted(set(range(n_sec)) - {m}, key=lambda to: (abs(to - m), -to))
            z = jnp.where(me == m, order[i], z)
        near.append(z)

    def nearest(visit):
        for z in near:
            visit(z)

    def load(src, dst, i):
        copy = pltpu.make_async_copy(src, dst, load_sem.at[i])
        copy.start()
        return copy

    barrier = pltpu.get_barrier_semaphore()
    for d in range(1, n_sec):
        pl.semaphore_signal(barrier, inc=1, device_id={"sec": sec_of(d)}, device_id_type=MESH)
    for peer in (x_peer, c_peer, d_peer):
        pl.semaphore_signal(barrier, inc=1, device_id=peer, device_id_type=MESH)

    columns = pl.ds(pl.multiple_of(core * kv_width, 128), kv_width)
    block = lambda z: pl.ds(pl.multiple_of(z * rows, rows), rows)
    load_k = load(keys.at[:, columns], kv.at[block(me), :], 0)
    load_v = load(values.at[:, columns], vv.at[block(me), :], 1)
    load_ids = load(ids, idsv, 2)
    load_codes = load(codes, codesv, 7)
    load_q = load(query, qv, 3)
    wov = wdv.at[pl.ds(0, out_weight.shape[0]), :]
    load_wo = load(out_weight, wov, 4)
    load_res = load(residual.at[pl.ds(pl.multiple_of(rank * own, own), own), :], resv, 5)
    load_gain = load(norm_gain, gainv, 6)
    weight_loads = []
    for which, (src, dst) in enumerate(((w_gate, wgv), (w_up, wuv), (w_down, wdv))):
        span = dst.shape[1] // WEIGHT_CHUNKS
        loads = []
        for i in range(WEIGHT_CHUNKS):
            piece = pl.ds(i * span, span)
            copy = pltpu.make_async_copy(
                src.at[0, :, piece], dst.at[:, piece], w_sem.at[which, i]
            )
            loads.append(copy)
        weight_loads.append(loads)

    for z in range(n_sec):

        @pl.when((z > me) | (z < me - reach))
        def _():
            kv[z * rows : (z + 1) * rows, :] = jnp.zeros((rows, kv_width), bf16)
            vv[z * rows : (z + 1) * rows, :] = jnp.zeros((rows, kv_width), bf16)

    load_k.wait()
    load_v.wait()
    pl.semaphore_wait(barrier, n_sec + 2)

    def kv_copy(which, ref, d, z, device):
        return rcopy(
            ref.at[block(z), :],
            ref.at[block(z), :],
            kv_send.at[which, d],
            kv_recv.at[which, z],
            device,
        )

    for which, ref in enumerate((kv, vv)):
        for d in range(1, reach + 1):

            @pl.when(me + d < n_sec)
            def _():
                kv_copy(which, ref, d, me, {"sec": sec_of(d)}).start()

    load_ids.wait()
    load_codes.wait()
    given = jnp.concatenate(
        [idsv[...].astype(f32), codesv[...].astype(f32), jnp.zeros((4, rows), f32)], axis=0
    )
    lane = lax.broadcasted_iota(jnp.int32, (rows, tokens), 1)
    row_of = (
        lax.rem(lane // quarter, 2) * (2 * own) + lane // half * own + lax.rem(lane, own)
    )
    here_z = lax.rem(lane, quarter) // own == me
    spread = jnp.where(
        here_z & (row_of == lax.broadcasted_iota(jnp.int32, (rows, tokens), 0)), 1.0, 0.0
    )
    routev[me] = jnp.dot(given.astype(bf16), spread.astype(bf16), preferred_element_type=f32)

    def route_copy(d, z):
        return rcopy(
            routev.at[z], routev.at[z], route_send.at[d], route_recv.at[z], {"sec": sec_of(d)}
        )

    for d in range(1, n_sec):
        route_copy(d, me).start()

    for i in range(WEIGHT_CHUNKS):
        weight_loads[0][i].start()
        weight_loads[1][i].start()

    load_q.wait()
    shape = (rows, tokens)
    query_pos = lax.broadcasted_iota(jnp.int32, shape, 0) + me * rows
    key_pos = lax.broadcasted_iota(jnp.int32, shape, 1)
    query_doc = jnp.zeros(shape, jnp.int32)
    key_doc = jnp.zeros(shape, jnp.int32)
    end = jnp.int32(0)
    for i in range(docs):
        end = end + lengths[i]
        query_doc += (query_pos >= end).astype(jnp.int32)
        key_doc += (key_pos >= end).astype(jnp.int32)
    allowed = jnp.where((key_pos <= query_pos) & (query_doc == key_doc), 1.0, 0.0)
    size = HEAD_DIMENSION
    group_width = QUERY_HEAD_COUNT // KEY_VALUE_HEADS
    allowed = jnp.concatenate([allowed] * group_width, axis=0) > 0.5

    def arrived(which, ref):
        for z in range(n_sec - 1):

            @pl.when((z < me) & (z >= me - reach))
            def _():
                kv_copy(which, ref, 1, z, {"sec": sec_of(1)}).wait_recv()

    arrived(0, kv)
    weights = []
    for g in range(kv_width // size):
        heads = range(g * group_width, (g + 1) * group_width)
        q = jnp.concatenate([qv[:, h * size : (h + 1) * size] for h in heads], axis=0)
        k = kv[:, g * size : (g + 1) * size]
        scores = lax.dot_general(
            q, k, (((1,), (1,)), ((), ())), preferred_element_type=f32
        ) * (size ** (-0.5))
        scores = jnp.where(allowed, scores, neg_fill)
        top = jnp.max(scores, axis=1, keepdims=True)
        probs = jnp.where(allowed, jnp.exp(scores - top), 0.0)
        total = jnp.sum(probs, axis=1, keepdims=True)
        weights.append((probs.astype(bf16), total))
    arrived(1, vv)
    for g, (probs, total) in enumerate(weights):
        heads = range(g * group_width, (g + 1) * group_width)
        v = vv[:, g * size : (g + 1) * size]
        mixed = jnp.dot(probs, v, preferred_element_type=f32) / total
        mixed = mixed.astype(bf16)
        for i, h in enumerate(heads):
            attv[:, h * size : (h + 1) * size] = mixed[i * rows : (i + 1) * rows, :]

    load_wo.wait()
    gather_span = width // GATHER_CHUNKS
    own_at = lambda r: pl.ds(pl.multiple_of(r * own, own), own)
    mix_from = (
        (d_peer, (1 - tx) * 2 + 1 - core),
        (x_peer, (1 - tx) * 2 + core),
        (c_peer, tx * 2 + 1 - core),
    )

    def mix_copy(i, k):
        peer, target = mix_from[i]
        at = pl.ds(k * gather_span, gather_span)
        return rcopy(
            part.at[own_at(target), at],
            mixin.at[i, :, at],
            mix_send.at[i, k],
            mix_recv.at[i, k],
            peer,
        )

    for k in range(GATHER_CHUNKS):
        at = slice(k * gather_span, (k + 1) * gather_span)
        part[:, at] = jnp.dot(attv[...], wov[:, at], preferred_element_type=f32).astype(bf16)
        for i in range(3):
            mix_copy(i, k).start()
    for copy in weight_loads[2]:
        copy.start()

    for d in range(1, n_sec):
        route_copy(d, sec_of(d)).wait_recv()
    facts = routev[0]
    for z in range(1, n_sec):
        facts = facts + routev[z]
    here = E // n_sec
    capacity = n_sec * MOSTB
    first, second = facts[0:1, :], facts[1:2, :]
    code_a, code_b = facts[2:3, :], facts[3:4, :]
    base = (me * here).astype(f32)
    local = lax.broadcasted_iota(jnp.int32, (8, tokens), 0).astype(f32) + base
    member = jnp.where((first == local) | (second == local), 1.0, 0.0)
    before = jnp.where(
        lax.broadcasted_iota(jnp.int32, (tokens, tokens), 0)
        < lax.broadcasted_iota(jnp.int32, (tokens, tokens), 1),
        1.0,
        0.0,
    ).astype(bf16)
    standing = jnp.dot(member.astype(bf16), before, preferred_element_type=f32)
    slot = lax.broadcasted_iota(jnp.int32, (capacity, tokens), 0).astype(f32)
    picks = []
    for e in range(here):
        pick = jnp.where((standing[e : e + 1, :] == slot) & (member[e : e + 1, :] > 0.5), 1.0, 0.0)
        coef = jnp.where(first == base + e, code_a, 0.0) + jnp.where(second == base + e, code_b, 0.0)
        coef = coef / (code_a + code_b)
        share = jnp.sum(pick * coef, axis=1, keepdims=True)
        sharev[e * capacity : (e + 1) * capacity, :] = jnp.broadcast_to(share, (capacity, 128))
        picks.append(pick)
    pick = jnp.concatenate(picks, axis=0)
    pickv[...] = pick.astype(bf16)
    pickt[...] = jnp.transpose(pick).astype(bf16)


    load_res.wait()
    load_gain.wait()
    spot = lambda c, x, z: pl.ds(
        pl.multiple_of(c * half + x * quarter + z * own, own), own
    )
    mine = spot(core, tx, me)
    gather_at = lambda k: pl.ds(
        k * gather_span, gather_span + (LANES if k == GATHER_CHUNKS - 1 else 0)
    )

    def nz_copy(to, z, k):
        at = nall.at[spot(core, tx, z), gather_at(k)]
        return rcopy(at, at, nz_send.at[to, k], nz_recv.at[z, k], {"sec": to})

    def nx_copy(x, z, k):
        at = nall.at[spot(core, x, z), gather_at(k)]
        return rcopy(at, at, nx_send.at[z, k], nx_recv.at[z, k], x_peer)

    def nc_copy(c, x, k):
        start = pl.multiple_of(c * half + x * quarter, quarter)
        at = nall.at[pl.ds(start, quarter), gather_at(k)]
        return rcopy(at, at, nc_send.at[x, k], nc_recv.at[x, k], c_peer)

    squares = jnp.zeros((own, 1), f32)
    for k in range(GATHER_CHUNKS):
        at = slice(k * gather_span, (k + 1) * gather_span)
        for i in range(3):
            mix_copy(i, k).wait_recv()
        total = part[own_at(rank), at].astype(f32)
        for i in range(3):
            total = total + mixin[i, :, at].astype(f32)
        total = total + resv[:, at].astype(f32)
        stream[:, at] = total
        squares = squares + jnp.sum(total * total, axis=1, keepdims=True)
        nall[mine, at] = (total * gainv[:, at]).astype(bf16)
        if k == GATHER_CHUNKS - 1:
            left = jnp.broadcast_to(lax.rsqrt(squares / width + norm_eps), (own, LANES))
            lane = lax.broadcasted_iota(jnp.int32, (own, LANES), 1)
            parts = jnp.zeros((own, LANES), f32)
            for i in range(3):
                now = left.astype(bf16).astype(f32)
                parts = jnp.where(lane == i, now, parts)
                left = left - now
            nall[mine, width:] = parts.astype(bf16)
        for z in near[::-1]:
            nz_copy(z, me, k).start()
        nx_copy(tx, me, k).start()

    def from_z(k):
        def visit(z):
            nz_copy(z, z, k).wait_recv()
            nx_copy(tx, z, k).start()

        for z in near[::-1]:
            visit(z)
        nc_copy(core, tx, k).start()

    def from_x(k):
        for z in range(n_sec):
            nx_copy(1 - tx, z, k).wait_recv()
        nc_copy(core, 1 - tx, k).start()

    def pack(k):
        for x in (tx, 1 - tx):
            nc_copy(1 - core, x, k).wait_recv()
        got = jnp.dot(pickv[...], nall[:, gather_at(k)], preferred_element_type=f32)
        packed[:, : got.shape[1]] = got.astype(bf16)

    units = wgv.shape[1] // here

    def expand(e, k):
        slots = slice(e * capacity, (e + 1) * capacity)
        of = slice(e * units, (e + 1) * units)
        at = slice(k * gather_span, (k + 1) * gather_span)
        x = packed[slots, :gather_span]
        gate = jnp.dot(x, wgv[at, of], preferred_element_type=f32)
        up = jnp.dot(x, wuv[at, of], preferred_element_type=f32)
        if k:
            gate = gate + gacc[slots, :]
            up = up + uacc[slots, :]
        if k < GATHER_CHUNKS - 1:
            gacc[slots, :] = gate
            uacc[slots, :] = up
            return
        scale = jnp.sum(
            packed[slots, gather_span : gather_span + LANES].astype(f32), axis=1, keepdims=True
        )
        gate = gate * scale
        act = gate / (1.0 + jnp.exp(-gate)) * (up * scale)
        hidden[slots, :] = act.astype(bf16)

    arrivals = [functools.partial(from_z, k) for k in range(GATHER_CHUNKS)]
    arrivals += [functools.partial(from_x, k) for k in range(GATHER_CHUNKS)]

    def forward(count):
        for step in arrivals[:count]:
            step()
        del arrivals[:count]

    forward(6)
    for copy in weight_loads[0] + weight_loads[1]:
        copy.wait()
    for k in range(GATHER_CHUNKS):
        pack(k)
        for e in range(here):
            expand(e, k)
            forward(1)

    for k in range(GATHER_CHUNKS):
        nearest(lambda z, k=k: nz_copy(z, me, k).wait_send())
        for z in range(n_sec):
            nx_copy(tx, z, k).wait_send()
        for x in (tx, 1 - tx):
            nc_copy(core, x, k).wait_send()
    for copy in weight_loads[2]:
        copy.wait()
    pout, acc = nall, gacc
    edges = [0]
    for eighths in RETURN_EIGHTHS:
        edges.append(edges[-1] + eighths * width // sum(RETURN_EIGHTHS))
    chunks = len(RETURN_EIGHTHS)
    return_at = lambda c: slice(edges[c], edges[c + 1])
    span_at = lambda c: pl.ds(edges[c], edges[c + 1] - edges[c])

    def shrink(c):
        at = return_at(c)
        outs = []
        for e in range(here):
            slots = slice(e * capacity, (e + 1) * capacity)
            y = jnp.dot(
                hidden[slots, :],
                wdv[e * units : (e + 1) * units, at],
                preferred_element_type=f32,
            )
            outs.append((y * sharev[slots, 0:1]).astype(bf16))
        y = jnp.concatenate(outs, axis=0)
        pout[:, at] = jnp.dot(pickt[...], y, preferred_element_type=f32).astype(bf16)

    half_at = lambda c: pl.ds(pl.multiple_of(c * half, half), half)
    quarter_at = lambda x: pl.ds(pl.multiple_of(x * quarter, quarter), quarter)

    def c1_copy(c):
        at = span_at(c)
        return rcopy(
            pout.at[half_at(1 - core), at], r1.at[:, at], c1_send.at[c], c1_recv.at[c], c_peer
        )

    def x2_copy(c):
        at = span_at(c)
        return rcopy(x_out.at[:, at], r2.at[:, at], x2_send.at[c], x2_recv.at[c], x_peer)

    def z3_copy(c, d, z, device):
        at = span_at(c)
        return rcopy(
            z_out.at[own_at(sec_of(d)), at],
            r3.at[own_at(z), at],
            z3_send.at[c, d],
            z3_recv.at[c, z],
            device,
        )

    def cross_core(c):
        at = return_at(c)
        c1_copy(c).wait_recv()
        other = pl.ds(pl.multiple_of(core * half + (1 - tx) * quarter, quarter), quarter)
        same = pl.ds(pl.multiple_of(core * half + tx * quarter, quarter), quarter)
        x_out[:, at] = (
            pout[other, at].astype(f32) + r1[quarter_at(1 - tx), at].astype(f32)
        ).astype(bf16)
        x2_copy(c).start()
        acc[:quarter, at] = pout[same, at].astype(f32) + r1[quarter_at(tx), at].astype(f32)

    def cross_x(c):
        at = return_at(c)
        x2_copy(c).wait_recv()
        total = acc[:quarter, at] + r2[:, at].astype(f32)
        acc[:quarter, at] = total
        z_out[:, at] = total.astype(bf16)
        for d in range(n_sec - 1, 0, -1):
            z3_copy(c, d, me, {"sec": sec_of(d)}).start()

    def cross_z(c):
        at = return_at(c)
        total = stream[:, at] + acc[own_at(me), at]
        for d in range(1, n_sec):
            z = sec_of(d)
            z3_copy(c, d, z, {"sec": z}).wait_recv()
            total = total + r3[own_at(z), at].astype(f32)
        out[:, at] = total.astype(bf16)

    for c in range(chunks):
        shrink(c)
        c1_copy(c).start()
        if c:
            cross_core(c - 1)
    cross_core(chunks - 1)
    for c in range(chunks):
        cross_x(c)
    for c in range(chunks):
        cross_z(c)

    for which, ref in enumerate((kv, vv)):
        for d in range(1, reach + 1):

            @pl.when(me + d < n_sec)
            def _():
                kv_copy(which, ref, d, me, {"sec": sec_of(d)}).wait_send()

    for d in range(1, n_sec):
        route_copy(d, me).wait_send()
    for i in range(3):
        for k in range(GATHER_CHUNKS):
            mix_copy(i, k).wait_send()
    for c in range(chunks):
        c1_copy(c).wait_send()
        x2_copy(c).wait_send()
        for d in range(1, n_sec):
            z3_copy(c, d, me, {"sec": sec_of(d)}).wait_send()


def fused_device(
    query,
    keys,
    values,
    residual,
    out_weight,
    norm_gain,
    expert_ids,
    gate_codes,
    doc_lengths,
    w_gate,
    w_up,
    w_down,
):
    n_sec = lax.axis_size("sec")
    rows, width = residual.shape
    own = rows // 4
    tokens = n_sec * rows
    here = E // n_sec
    slots = here * n_sec * MOSTB
    kv_width = query.shape[1] * KEY_VALUE_HEADS // QUERY_HEAD_COUNT
    f32, bf16 = jnp.float32, jnp.bfloat16
    V, dma = pltpu.VMEM, pltpu.SemaphoreType.DMA
    anywhere = pl.BlockSpec(memory_space=pl.ANY)
    return pl.pallas_call(
        functools.partial(layer_kernel, n_sec, doc_lengths.shape[0]),
        out_shape=pltpu.VMEM((own, width), bf16),
        in_specs=[pl.BlockSpec(memory_space=pltpu.SMEM)] + [anywhere] * 11,
        out_specs=pl.BlockSpec(memory_space=pltpu.VMEM),
        scratch_shapes=[
            V(query.shape, bf16),
            V((tokens, kv_width), bf16),
            V((tokens, kv_width), bf16),
            V(query.shape, bf16),
            V((own, width), bf16),
            V((1, width), f32),
            V(expert_ids.shape[::-1], jnp.int32),
            V(gate_codes.shape[::-1], jnp.int32),
            V((n_sec, 8, tokens), f32),
            V(w_gate.shape[1:], bf16),
            V(w_up.shape[1:], bf16),
            V(w_down.shape[1:], bf16),
            V((rows, width), bf16),
            V((3, own, width), bf16),
            V((own, width), f32),
            V((tokens, width + LANES), bf16),
            V((slots, width // GATHER_CHUNKS + LANES), bf16),
            V((slots, w_gate.shape[2] // here), f32),
            V((slots, w_gate.shape[2] // here), f32),
            V((slots, w_gate.shape[2] // here), bf16),
            V((slots, tokens), bf16),
            V((tokens, slots), bf16),
            V((slots, LANES), f32),
            V((tokens // 2, width), bf16),
            V((tokens // 4, width), bf16),
            V((tokens // 4, width), bf16),
            V((tokens // 4, width), bf16),
            V((tokens // 4, width), bf16),
            dma((8,)),
            dma((3, WEIGHT_CHUNKS)),
            dma((2, n_sec)),
            dma((2, n_sec)),
            dma((n_sec,)),
            dma((n_sec,)),
            *[dma((3, GATHER_CHUNKS))] * 2,
            *[dma((n_sec, GATHER_CHUNKS))] * 4,
            *[dma((2, GATHER_CHUNKS))] * 2,
            *[dma((len(RETURN_EIGHTHS),))] * 4,
            *[dma((len(RETURN_EIGHTHS), n_sec))] * 2,
        ],
        compiler_params=pltpu.CompilerParams(
            collective_id=0, has_side_effects=True, vmem_limit_bytes=66900000
        ),
    )(
        doc_lengths,
        query,
        keys,
        values,
        residual,
        out_weight,
        norm_gain.reshape(1, width),
        expert_ids.T,
        gate_codes.T,
        w_gate,
        w_up,
        w_down,
    )


def whole_in_vmem(mesh):
    shape = mesh.shape
    return shape["tp"] == 2 and shape["pp"] == 2 and shape["sec"] > 1 and E % shape["sec"] == 0


def solution(mesh):
    in_specs = (
        P(("groups", "sec"), ("tp", "pp")),
        P(("groups", "sec"), "tp"),
        P(("groups", "sec"), "tp"),
        P(("groups", "sec"), None),
        P(("tp", "pp"), None),
        P(),
        P(("groups", "sec"), None),
        P(("groups", "sec"), None),
        P("groups"),
        P(("tp", "pp"), None, "sec"),
        P(("tp", "pp"), None, "sec"),
        P(("tp", "pp"), "sec", None),
    )
    out_specs = P(("groups", "sec", "tp", "pp"), None)
    return jax.shard_map(
        fused_device if whole_in_vmem(mesh) else per_device,
        mesh=mesh,
        in_specs=in_specs,
        out_specs=out_specs,
        check_vma=False,
    )
```

```python
import functools

import jax
import jax.numpy as jnp
from jax import lax
from jax.experimental import pallas as pl
from jax.experimental.pallas import tpu as pltpu
from jax.sharding import PartitionSpec as P

QUERY_HEAD_COUNT = 32
KEY_VALUE_HEADS = 8
HEAD_DIMENSION = 128
E = 8
MOSTB = 32


neg_fill = -1e30
norm_eps = 1e-05


def doc_index(positions, doc_ends):
    return jnp.sum((positions[:, None] >= doc_ends[None, :]).astype(jnp.int32), axis=1)


def running_sum(counts):
    order = jnp.arange(counts.shape[0], dtype=jnp.int32)
    upto = (order[None, :] <= order[:, None]).reshape(order.shape * 2 + (1,) * (counts.ndim - 1))
    return jnp.sum(jnp.where(upto, counts[None], 0), axis=1)


def rms_scale(stream, norm_gain):
    meansq = jnp.mean(stream * stream, axis=1, keepdims=True)
    return (stream * lax.rsqrt(meansq + norm_eps) * norm_gain).astype(jnp.bfloat16)


def per_device(
    query,
    keys,
    values,
    residual,
    out_weight,
    norm_gain,
    expert_ids,
    gate_codes,
    doc_lengths,
    w_gate,
    w_up,
    w_down,
):
    block_rows = query.shape[0]
    head_size = HEAD_DIMENSION
    q_heads = query.shape[1] // head_size
    kv_heads = keys.shape[1] // head_size
    group_width = QUERY_HEAD_COUNT // KEY_VALUE_HEADS
    width = residual.shape[1]
    sec_count = lax.axis_size("sec")
    rank_count = lax.axis_size("tp") * lax.axis_size("pp")
    pp_index = lax.axis_index("pp")
    rank_index = lax.axis_index("tp") * lax.axis_size("pp") + pp_index
    own_rows = block_rows // rank_count
    own_start = rank_index * own_rows
    doc_ends = running_sum(doc_lengths)
    query_pos = lax.axis_index("sec") * block_rows + jnp.arange(block_rows, dtype=jnp.int32)
    query_doc = doc_index(query_pos, doc_ends)
    kv_pick = (pp_index * q_heads + jnp.arange(q_heads, dtype=jnp.int32)) // group_width
    query_heads = query.reshape(block_rows, q_heads, head_size)
    scale = head_size ** (-0.5)
    run_max = jnp.full((q_heads, block_rows), neg_fill, jnp.float32)
    key_piece = lax.all_gather(keys, "sec", axis=0, tiled=True)
    value_piece = lax.all_gather(values, "sec", axis=0, tiled=True)
    count = key_piece.shape[0]
    key_heads = jnp.take(key_piece.reshape(count, kv_heads, head_size), kv_pick, axis=1)
    value_heads = jnp.take(value_piece.reshape(count, kv_heads, head_size), kv_pick, axis=1)
    scores = (
        jnp.einsum("qhd,khd->hqk", query_heads, key_heads, preferred_element_type=jnp.float32)
        * scale
    )
    key_pos = jnp.arange(count, dtype=jnp.int32)
    allowed = (key_pos[None, :] <= query_pos[:, None]) & (
        doc_index(key_pos, doc_ends)[None, :] == query_doc[:, None]
    )
    scores = jnp.where(allowed[None], scores, neg_fill)
    new_max = jnp.maximum(run_max, jnp.max(scores, axis=2))
    probs = jnp.where(allowed[None], jnp.exp(scores - new_max[:, :, None]), 0.0)
    run_total = jnp.sum(probs, axis=2)
    run_acc = jnp.einsum(
        "hqk,khd->hqd", probs.astype(jnp.bfloat16), value_heads, preferred_element_type=jnp.float32
    )
    run_max, run_total, run_acc = (new_max, run_total, run_acc)
    attended = (
        (run_acc / run_total[:, :, None])
        .transpose(1, 0, 2)
        .reshape(block_rows, q_heads * head_size)
        .astype(jnp.bfloat16)
    )
    rows_in = attended
    mixed_own = lax.psum_scatter(
        jnp.dot(rows_in, out_weight, preferred_element_type=jnp.float32).astype(jnp.bfloat16),
        ("tp", "pp"),
        scatter_dimension=0,
        tiled=True,
    ).astype(jnp.float32)
    stream_own = (
        lax.dynamic_slice_in_dim(residual, own_start, own_rows, 0).astype(jnp.float32) + mixed_own
    )
    normed = lax.all_gather(rms_scale(stream_own, norm_gain), ("tp", "pp"), axis=0, tiled=True)
    capacity = MOSTB
    experts_here = max(1, E // sec_count)
    halves = max(1, sec_count // E)
    route_hits = (expert_ids[:, :, None] == jnp.arange(E, dtype=jnp.int32)[None, None, :]).astype(
        jnp.int32
    )
    member = jnp.sum(route_hits, axis=1)
    slots = running_sum(member) - 1
    slot_pick = jnp.sum(route_hits * slots[:, None, :], axis=2)
    codes = gate_codes.astype(jnp.float32)
    shares = codes / jnp.sum(codes, axis=1, keepdims=True)
    slot_range = jnp.arange(capacity, dtype=jnp.int32)
    select = (
        (slots.T[:, None, :] == slot_range[None, :, None]) & (member.T[:, None, :] == 1)
    ).astype(jnp.bfloat16)
    gate_local = w_gate[0].reshape(width, experts_here, -1)
    up_local = w_up[0].reshape(width, experts_here, -1)
    down_local = w_down[0].reshape(experts_here, -1, width)
    packed = jnp.einsum("ecr,rd->ecd", select, normed, preferred_element_type=jnp.float32).astype(
        jnp.bfloat16
    )
    packed = jnp.repeat(packed, halves, axis=0)
    rows_in = lax.all_to_all(
        packed.reshape(sec_count, experts_here, capacity, normed.shape[1]),
        "sec",
        split_axis=0,
        concat_axis=0,
        tiled=True,
    )
    gate = jnp.einsum("sxmd,dxf->sxmf", rows_in, gate_local, preferred_element_type=jnp.float32)
    up = jnp.einsum("sxmd,dxf->sxmf", rows_in, up_local, preferred_element_type=jnp.float32)
    hidden = (jax.nn.silu(gate) * up).astype(jnp.bfloat16)
    partial_out = jnp.einsum(
        "sxmf,xfd->sxmd", hidden, down_local, preferred_element_type=jnp.float32
    )
    returned = lax.all_to_all(
        partial_out.astype(jnp.bfloat16), "sec", split_axis=0, concat_axis=0, tiled=True
    ).astype(partial_out.dtype)
    flat_parts = returned.reshape(sec_count * experts_here * capacity, width)
    half_range = jnp.arange(halves, dtype=jnp.int32)
    top_count = expert_ids.shape[1]
    index = ((expert_ids * halves)[:, :, None] + half_range[None, None, :]) * capacity + slot_pick[
        :, :, None
    ]
    picked = jnp.take(flat_parts, index.reshape(-1), axis=0).reshape(
        own_rows * lax.axis_size(("tp", "pp")), top_count, halves, width
    )
    mixture_own = lax.psum_scatter(
        jnp.sum(picked * shares[:, :, None, None], axis=(1, 2)).astype(jnp.bfloat16),
        ("tp", "pp"),
        scatter_dimension=0,
        tiled=True,
    ).astype(jnp.float32)
    return (stream_own + mixture_own).astype(jnp.bfloat16)


MESH = pl.DeviceIdType.MESH
LANES = 128
GATHER_CHUNKS = 4
RETURN_EIGHTHS = (2, 2, 2, 2)
AHEAD_AFTER = 2
WEIGHT_CHUNKS = 4


def rcopy(src, dst, send_sem, recv_sem, device):
    return pltpu.make_async_remote_copy(
        src_ref=src,
        dst_ref=dst,
        send_sem=send_sem,
        recv_sem=recv_sem,
        device_id=device,
        device_id_type=MESH,
    )


def layer_kernel(
    n_sec,
    docs,
    lengths,
    query,
    keys,
    values,
    residual,
    out_weight,
    norm_gain,
    ids,
    codes,
    w_gate,
    w_up,
    w_down,
    out,
    qv,
    kv,
    vv,
    attv,
    resv,
    gainv,
    idsv,
    codesv,
    routev,
    wgv,
    wuv,
    wdv,
    part,
    mixin,
    stream,
    nall,
    packed,
    gacc,
    uacc,
    hidden,
    pickv,
    pickt,
    sharev,
    r1,
    x_out,
    r2,
    z_out,
    r3,
    ahead_out,
    ahead_in,
    cross_out,
    cross_in,
    load_sem,
    w_sem,
    kv_send,
    kv_recv,
    route_send,
    route_recv,
    mix_send,
    mix_recv,
    nz_send,
    nz_recv,
    nx_send,
    nx_recv,
    nc_send,
    nc_recv,
    c1_send,
    c1_recv,
    x2_send,
    x2_recv,
    z3_send,
    z3_recv,
    ahead_send,
    ahead_recv,
    cross_send,
    cross_recv,
):
    f32, bf16 = jnp.float32, jnp.bfloat16
    me, tx, core = lax.axis_index("sec"), lax.axis_index("tp"), lax.axis_index("pp")
    rank = tx * 2 + core
    rows, width = residual.shape
    own = rows // 4
    kv_width = kv.shape[1]
    tokens = n_sec * rows
    half, quarter = tokens // 2, tokens // 4
    x_peer, c_peer = {"tp": 1 - tx}, {"pp": 1 - core}
    d_peer = {"tp": 1 - tx, "pp": 1 - core}
    sec_of = lambda d: lax.rem(me + d, n_sec)
    longest = tokens // 2
    reach = min(n_sec - 1, pl.cdiv(longest - 1, rows))

    near = []
    for i in range(n_sec - 1):
        z = jnp.int32(0)
        for m in range(n_sec):
            order = sorted(set(range(n_sec)) - {m}, key=lambda to: (abs(to - m), -to))
            z = jnp.where(me == m, order[i], z)
        near.append(z)

    def nearest(visit):
        for z in near:
            visit(z)

    def load(src, dst, i):
        copy = pltpu.make_async_copy(src, dst, load_sem.at[i])
        copy.start()
        return copy

    barrier = pltpu.get_barrier_semaphore()
    for d in range(1, n_sec):
        pl.semaphore_signal(barrier, inc=1, device_id={"sec": sec_of(d)}, device_id_type=MESH)
    for peer in (x_peer, c_peer, d_peer):
        pl.semaphore_signal(barrier, inc=1, device_id=peer, device_id_type=MESH)

    columns = pl.ds(pl.multiple_of(core * kv_width, 128), kv_width)
    block = lambda z: pl.ds(pl.multiple_of(z * rows, rows), rows)
    load_k = load(keys.at[:, columns], kv.at[block(me), :], 0)
    load_v = load(values.at[:, columns], vv.at[block(me), :], 1)
    load_ids = load(ids, idsv, 2)
    load_codes = load(codes, codesv, 7)
    load_q = load(query, qv, 3)
    wov = wdv.at[pl.ds(0, out_weight.shape[0]), :]
    load_wo = load(out_weight, wov, 4)
    load_res = load(residual.at[pl.ds(pl.multiple_of(rank * own, own), own), :], resv, 5)
    load_gain = load(norm_gain, gainv, 6)
    weight_loads = []
    for which, (src, dst) in enumerate(((w_gate, wgv), (w_up, wuv), (w_down, wdv))):
        span = dst.shape[1] // WEIGHT_CHUNKS
        loads = []
        for i in range(WEIGHT_CHUNKS):
            piece = pl.ds(i * span, span)
            copy = pltpu.make_async_copy(
                src.at[0, :, piece], dst.at[:, piece], w_sem.at[which, i]
            )
            loads.append(copy)
        weight_loads.append(loads)

    for z in range(n_sec):

        @pl.when((z > me) | (z < me - reach))
        def _():
            kv[z * rows : (z + 1) * rows, :] = jnp.zeros((rows, kv_width), bf16)
            vv[z * rows : (z + 1) * rows, :] = jnp.zeros((rows, kv_width), bf16)

    load_k.wait()
    load_v.wait()
    pl.semaphore_wait(barrier, n_sec + 2)

    def kv_copy(which, ref, d, z, device):
        return rcopy(
            ref.at[block(z), :],
            ref.at[block(z), :],
            kv_send.at[which, d],
            kv_recv.at[which, z],
            device,
        )

    for which, ref in enumerate((kv, vv)):
        for d in range(1, reach + 1):

            @pl.when(me + d < n_sec)
            def _():
                kv_copy(which, ref, d, me, {"sec": sec_of(d)}).start()

    load_ids.wait()
    load_codes.wait()
    given = jnp.concatenate(
        [idsv[...].astype(f32), codesv[...].astype(f32), jnp.zeros((4, rows), f32)], axis=0
    )
    lane = lax.broadcasted_iota(jnp.int32, (rows, tokens), 1)
    row_of = (
        lax.rem(lane // quarter, 2) * (2 * own) + lane // half * own + lax.rem(lane, own)
    )
    here_z = lax.rem(lane, quarter) // own == me
    spread = jnp.where(
        here_z & (row_of == lax.broadcasted_iota(jnp.int32, (rows, tokens), 0)), 1.0, 0.0
    )
    routev[me] = jnp.dot(given.astype(bf16), spread.astype(bf16), preferred_element_type=f32)

    def route_copy(d, z):
        return rcopy(
            routev.at[z], routev.at[z], route_send.at[d], route_recv.at[z], {"sec": sec_of(d)}
        )

    for d in range(1, n_sec):
        route_copy(d, me).start()

    for i in range(WEIGHT_CHUNKS):
        weight_loads[0][i].start()
        weight_loads[1][i].start()

    load_q.wait()
    shape = (rows, tokens)
    query_pos = lax.broadcasted_iota(jnp.int32, shape, 0) + me * rows
    key_pos = lax.broadcasted_iota(jnp.int32, shape, 1)
    query_doc = jnp.zeros(shape, jnp.int32)
    key_doc = jnp.zeros(shape, jnp.int32)
    end = jnp.int32(0)
    for i in range(docs):
        end = end + lengths[i]
        query_doc += (query_pos >= end).astype(jnp.int32)
        key_doc += (key_pos >= end).astype(jnp.int32)
    allowed = jnp.where((key_pos <= query_pos) & (query_doc == key_doc), 1.0, 0.0)
    size = HEAD_DIMENSION
    group_width = QUERY_HEAD_COUNT // KEY_VALUE_HEADS
    allowed = jnp.concatenate([allowed] * group_width, axis=0) > 0.5

    def arrived(which, ref):
        for z in range(n_sec - 1):

            @pl.when((z < me) & (z >= me - reach))
            def _():
                kv_copy(which, ref, 1, z, {"sec": sec_of(1)}).wait_recv()

    arrived(0, kv)
    weights = []
    for g in range(kv_width // size):
        heads = range(g * group_width, (g + 1) * group_width)
        q = jnp.concatenate([qv[:, h * size : (h + 1) * size] for h in heads], axis=0)
        k = kv[:, g * size : (g + 1) * size]
        scores = lax.dot_general(
            q, k, (((1,), (1,)), ((), ())), preferred_element_type=f32
        ) * (size ** (-0.5))
        scores = jnp.where(allowed, scores, neg_fill)
        top = jnp.max(scores, axis=1, keepdims=True)
        probs = jnp.where(allowed, jnp.exp(scores - top), 0.0)
        total = jnp.sum(probs, axis=1, keepdims=True)
        weights.append((probs.astype(bf16), total))
    arrived(1, vv)
    for g, (probs, total) in enumerate(weights):
        heads = range(g * group_width, (g + 1) * group_width)
        v = vv[:, g * size : (g + 1) * size]
        mixed = jnp.dot(probs, v, preferred_element_type=f32) / total
        mixed = mixed.astype(bf16)
        for i, h in enumerate(heads):
            attv[:, h * size : (h + 1) * size] = mixed[i * rows : (i + 1) * rows, :]

    load_wo.wait()
    gather_span = width // GATHER_CHUNKS
    own_at = lambda r: pl.ds(pl.multiple_of(r * own, own), own)
    mix_from = (
        (d_peer, (1 - tx) * 2 + 1 - core),
        (x_peer, (1 - tx) * 2 + core),
        (c_peer, tx * 2 + 1 - core),
    )

    def mix_copy(i, k):
        peer, target = mix_from[i]
        at = pl.ds(k * gather_span, gather_span)
        return rcopy(
            part.at[own_at(target), at],
            mixin.at[i, :, at],
            mix_send.at[i, k],
            mix_recv.at[i, k],
            peer,
        )

    for k in range(GATHER_CHUNKS):
        at = slice(k * gather_span, (k + 1) * gather_span)
        part[:, at] = jnp.dot(attv[...], wov[:, at], preferred_element_type=f32).astype(bf16)
        for i in range(3):
            mix_copy(i, k).start()
    for copy in weight_loads[2]:
        copy.start()

    for d in range(1, n_sec):
        route_copy(d, sec_of(d)).wait_recv()
    facts = routev[0]
    for z in range(1, n_sec):
        facts = facts + routev[z]
    here = E // n_sec
    capacity = n_sec * MOSTB
    first, second = facts[0:1, :], facts[1:2, :]
    code_a, code_b = facts[2:3, :], facts[3:4, :]
    base = (me * here).astype(f32)
    local = lax.broadcasted_iota(jnp.int32, (8, tokens), 0).astype(f32) + base
    member = jnp.where((first == local) | (second == local), 1.0, 0.0)
    before = jnp.where(
        lax.broadcasted_iota(jnp.int32, (tokens, tokens), 0)
        < lax.broadcasted_iota(jnp.int32, (tokens, tokens), 1),
        1.0,
        0.0,
    ).astype(bf16)
    standing = jnp.dot(member.astype(bf16), before, preferred_element_type=f32)
    slot = lax.broadcasted_iota(jnp.int32, (capacity, tokens), 0).astype(f32)
    picks = []
    for e in range(here):
        pick = jnp.where((standing[e : e + 1, :] == slot) & (member[e : e + 1, :] > 0.5), 1.0, 0.0)
        coef = jnp.where(first == base + e, code_a, 0.0) + jnp.where(second == base + e, code_b, 0.0)
        coef = coef / (code_a + code_b)
        share = jnp.sum(pick * coef, axis=1, keepdims=True)
        sharev[e * capacity : (e + 1) * capacity, :] = jnp.broadcast_to(share, (capacity, 128))
        picks.append(pick)
    pick = jnp.concatenate(picks, axis=0)
    pickv[...] = pick.astype(bf16)
    pickt[...] = jnp.transpose(pick).astype(bf16)


    load_res.wait()
    load_gain.wait()
    spot = lambda c, x, z: pl.ds(
        pl.multiple_of(c * half + x * quarter + z * own, own), own
    )
    mine = spot(core, tx, me)
    gather_at = lambda k: pl.ds(
        k * gather_span, gather_span + (LANES if k == GATHER_CHUNKS - 1 else 0)
    )

    def nz_copy(to, z, k):
        at = nall.at[spot(core, tx, z), gather_at(k)]
        return rcopy(at, at, nz_send.at[to, k], nz_recv.at[z, k], {"sec": to})

    def nx_copy(x, z, k):
        at = nall.at[spot(core, x, z), gather_at(k)]
        return rcopy(at, at, nx_send.at[z, k], nx_recv.at[z, k], x_peer)

    def nc_copy(c, x, k):
        start = pl.multiple_of(c * half + x * quarter, quarter)
        at = nall.at[pl.ds(start, quarter), gather_at(k)]
        return rcopy(at, at, nc_send.at[x, k], nc_recv.at[x, k], c_peer)

    squares = jnp.zeros((own, 1), f32)
    for k in range(GATHER_CHUNKS):
        at = slice(k * gather_span, (k + 1) * gather_span)
        for i in range(3):
            mix_copy(i, k).wait_recv()
        total = part[own_at(rank), at].astype(f32)
        for i in range(3):
            total = total + mixin[i, :, at].astype(f32)
        total = total + resv[:, at].astype(f32)
        stream[:, at] = total
        squares = squares + jnp.sum(total * total, axis=1, keepdims=True)
        nall[mine, at] = (total * gainv[:, at]).astype(bf16)
        if k == GATHER_CHUNKS - 1:
            left = jnp.broadcast_to(lax.rsqrt(squares / width + norm_eps), (own, LANES))
            lane = lax.broadcasted_iota(jnp.int32, (own, LANES), 1)
            parts = jnp.zeros((own, LANES), f32)
            for i in range(3):
                now = left.astype(bf16).astype(f32)
                parts = jnp.where(lane == i, now, parts)
                left = left - now
            nall[mine, width:] = parts.astype(bf16)
        for z in near[::-1]:
            nz_copy(z, me, k).start()
        nx_copy(tx, me, k).start()

    def from_z(k):
        def visit(z):
            nz_copy(z, z, k).wait_recv()
            nx_copy(tx, z, k).start()

        for z in near[::-1]:
            visit(z)
        nc_copy(core, tx, k).start()

    def from_x(k):
        for z in range(n_sec):
            nx_copy(1 - tx, z, k).wait_recv()
        nc_copy(core, 1 - tx, k).start()

    def pack(k):
        for x in (tx, 1 - tx):
            nc_copy(1 - core, x, k).wait_recv()
        got = jnp.dot(pickv[...], nall[:, gather_at(k)], preferred_element_type=f32)
        packed[:, : got.shape[1]] = got.astype(bf16)

    units = wgv.shape[1] // here

    def expand(e, k):
        slots = slice(e * capacity, (e + 1) * capacity)
        of = slice(e * units, (e + 1) * units)
        at = slice(k * gather_span, (k + 1) * gather_span)
        x = packed[slots, :gather_span]
        gate = jnp.dot(x, wgv[at, of], preferred_element_type=f32)
        up = jnp.dot(x, wuv[at, of], preferred_element_type=f32)
        if k:
            gate = gate + gacc[slots, :]
            up = up + uacc[slots, :]
        if k < GATHER_CHUNKS - 1:
            gacc[slots, :] = gate
            uacc[slots, :] = up
            return
        scale = jnp.sum(
            packed[slots, gather_span : gather_span + LANES].astype(f32), axis=1, keepdims=True
        )
        gate = gate * scale
        act = gate / (1.0 + jnp.exp(-gate)) * (up * scale)
        hidden[slots, :] = act.astype(bf16)

    arrivals = [functools.partial(from_z, k) for k in range(GATHER_CHUNKS)]
    arrivals += [functools.partial(from_x, k) for k in range(GATHER_CHUNKS)]

    def forward(count):
        for step in arrivals[:count]:
            step()
        del arrivals[:count]

    forward(6)
    for copy in weight_loads[0] + weight_loads[1]:
        copy.wait()
    for k in range(GATHER_CHUNKS):
        pack(k)
        for e in range(here):
            expand(e, k)
            forward(1)

    for k in range(GATHER_CHUNKS):
        nearest(lambda z, k=k: nz_copy(z, me, k).wait_send())
        for z in range(n_sec):
            nx_copy(tx, z, k).wait_send()
        for x in (tx, 1 - tx):
            nc_copy(core, x, k).wait_send()
    for copy in weight_loads[2]:
        copy.wait()
    pout, acc = nall, gacc
    edges = [0]
    for eighths in RETURN_EIGHTHS:
        edges.append(edges[-1] + eighths * width // sum(RETURN_EIGHTHS))
    chunks = len(RETURN_EIGHTHS)
    return_at = lambda c: slice(edges[c], edges[c + 1])
    span_at = lambda c: pl.ds(edges[c], edges[c + 1] - edges[c])

    def shrink(c):
        at = return_at(c)
        outs = []
        for e in range(here):
            slots = slice(e * capacity, (e + 1) * capacity)
            y = jnp.dot(
                hidden[slots, :],
                wdv[e * units : (e + 1) * units, at],
                preferred_element_type=f32,
            )
            outs.append((y * sharev[slots, 0:1]).astype(bf16))
        y = jnp.concatenate(outs, axis=0)
        pout[:, at] = jnp.dot(pickt[...], y, preferred_element_type=f32).astype(bf16)

    half_at = lambda c: pl.ds(pl.multiple_of(c * half, half), half)
    quarter_at = lambda x: pl.ds(pl.multiple_of(x * quarter, quarter), quarter)

    def c1_copy(c):
        at = span_at(c)
        return rcopy(
            pout.at[half_at(1 - core), at], r1.at[:, at], c1_send.at[c], c1_recv.at[c], c_peer
        )

    def x2_copy(c):
        at = span_at(c)
        return rcopy(x_out.at[:, at], r2.at[:, at], x2_send.at[c], x2_recv.at[c], x_peer)

    def z3_copy(c, d, z, device):
        at = span_at(c)
        return rcopy(
            z_out.at[own_at(sec_of(d)), at],
            r3.at[own_at(z), at],
            z3_send.at[c, d],
            z3_recv.at[c, z],
            device,
        )

    def cross_core(c):
        at = return_at(c)
        c1_copy(c).wait_recv()
        other = pl.ds(pl.multiple_of(core * half + (1 - tx) * quarter, quarter), quarter)
        same = pl.ds(pl.multiple_of(core * half + tx * quarter, quarter), quarter)
        x_out[:, at] = (
            pout[other, at].astype(f32) + r1[quarter_at(1 - tx), at].astype(f32)
        ).astype(bf16)
        x2_copy(c).start()
        acc[:quarter, at] = pout[same, at].astype(f32) + r1[quarter_at(tx), at].astype(f32)

    def cross_x(c):
        at = return_at(c)
        x2_copy(c).wait_recv()
        total = acc[:quarter, at] + r2[:, at].astype(f32)
        acc[:quarter, at] = total
        z_out[:, at] = total.astype(bf16)
        for d in range(n_sec - 1, 0, -1):
            z3_copy(c, d, me, {"sec": sec_of(d)}).start()

    def cross_z(c):
        at = return_at(c)
        total = stream[:, at] + acc[own_at(me), at]
        for d in range(1, n_sec):
            z = sec_of(d)
            z3_copy(c, d, z, {"sec": z}).wait_recv()
            total = total + r3[own_at(z), at].astype(f32)
        out[:, at] = total.astype(bf16)

    at_x = lambda x, z: pl.ds(pl.multiple_of(x * quarter + z * own, own), own)

    def ahead_copy(d, x, to, z, device):
        return rcopy(
            ahead_out.at[at_x(x, to), :],
            ahead_in.at[at_x(x, z), :],
            ahead_send.at[d, x],
            ahead_recv.at[z, x],
            device,
        )

    def cross_copy():
        return rcopy(cross_out, cross_in, cross_send.at[0], cross_recv.at[0], x_peer)

    def ahead_core():
        at = return_at(0)
        c1_copy(0).wait_recv()
        ahead_out[...] = (pout[half_at(core), at].astype(f32) + r1[:, at].astype(f32)).astype(bf16)
        for d in range(n_sec - 1, 0, -1):
            for x in range(2):
                ahead_copy(d, x, sec_of(d), me, {"sec": sec_of(d)}).start()

    def ahead_sum(x):
        at = return_at(0)
        start = pl.multiple_of(core * half + x * quarter + me * own, own)
        total = pout[pl.ds(start, own), at].astype(f32) + r1[at_x(x, me), at].astype(f32)
        for d in range(1, n_sec):
            total = total + ahead_in[at_x(x, sec_of(d)), :].astype(f32)
        return total

    def ahead_z():
        for d in range(1, n_sec):
            for x in range(2):
                ahead_copy(d, x, me, sec_of(d), {"sec": sec_of(d)}).wait_recv()
        cross_out[...] = ahead_sum(1 - tx).astype(bf16)
        cross_copy().start()
        acc[:own, return_at(0)] = ahead_sum(tx)

    def ahead_x():
        at = return_at(0)
        cross_copy().wait_recv()
        out[:, at] = (stream[:, at] + acc[:own, at] + cross_in[...].astype(f32)).astype(bf16)

    shrink(0)
    c1_copy(0).start()
    shrink(1)
    c1_copy(1).start()
    ahead_core()
    for c in range(2, chunks):
        shrink(c)
        c1_copy(c).start()
        cross_core(c - 1)
    cross_core(chunks - 1)
    for c in range(1, chunks):
        cross_x(c)
        if c == AHEAD_AFTER:
            ahead_z()
    ahead_x()
    for c in range(1, chunks):
        cross_z(c)

    for which, ref in enumerate((kv, vv)):
        for d in range(1, reach + 1):

            @pl.when(me + d < n_sec)
            def _():
                kv_copy(which, ref, d, me, {"sec": sec_of(d)}).wait_send()

    for d in range(1, n_sec):
        route_copy(d, me).wait_send()
    for i in range(3):
        for k in range(GATHER_CHUNKS):
            mix_copy(i, k).wait_send()
    for d in range(1, n_sec):
        for x in range(2):
            ahead_copy(d, x, sec_of(d), me, {"sec": sec_of(d)}).wait_send()
    cross_copy().wait_send()
    for c in range(chunks):
        c1_copy(c).wait_send()
    for c in range(1, chunks):
        x2_copy(c).wait_send()
        for d in range(1, n_sec):
            z3_copy(c, d, me, {"sec": sec_of(d)}).wait_send()


def fused_device(
    query,
    keys,
    values,
    residual,
    out_weight,
    norm_gain,
    expert_ids,
    gate_codes,
    doc_lengths,
    w_gate,
    w_up,
    w_down,
):
    n_sec = lax.axis_size("sec")
    rows, width = residual.shape
    own = rows // 4
    tokens = n_sec * rows
    here = E // n_sec
    slots = here * n_sec * MOSTB
    ahead = RETURN_EIGHTHS[0] * width // sum(RETURN_EIGHTHS)
    kv_width = query.shape[1] * KEY_VALUE_HEADS // QUERY_HEAD_COUNT
    f32, bf16 = jnp.float32, jnp.bfloat16
    V, dma = pltpu.VMEM, pltpu.SemaphoreType.DMA
    anywhere = pl.BlockSpec(memory_space=pl.ANY)
    return pl.pallas_call(
        functools.partial(layer_kernel, n_sec, doc_lengths.shape[0]),
        out_shape=pltpu.VMEM((own, width), bf16),
        in_specs=[pl.BlockSpec(memory_space=pltpu.SMEM)] + [anywhere] * 11,
        out_specs=pl.BlockSpec(memory_space=pltpu.VMEM),
        scratch_shapes=[
            V(query.shape, bf16),
            V((tokens, kv_width), bf16),
            V((tokens, kv_width), bf16),
            V(query.shape, bf16),
            V((own, width), bf16),
            V((1, width), f32),
            V(expert_ids.shape[::-1], jnp.int32),
            V(gate_codes.shape[::-1], jnp.int32),
            V((n_sec, 8, tokens), f32),
            V(w_gate.shape[1:], bf16),
            V(w_up.shape[1:], bf16),
            V(w_down.shape[1:], bf16),
            V((rows, width), bf16),
            V((3, own, width), bf16),
            V((own, width), f32),
            V((tokens, width + LANES), bf16),
            V((slots, width // GATHER_CHUNKS + LANES), bf16),
            V((slots, w_gate.shape[2] // here), f32),
            V((slots, w_gate.shape[2] // here), f32),
            V((slots, w_gate.shape[2] // here), bf16),
            V((slots, tokens), bf16),
            V((tokens, slots), bf16),
            V((slots, LANES), f32),
            V((tokens // 2, width), bf16),
            V((tokens // 4, width), bf16),
            V((tokens // 4, width), bf16),
            V((tokens // 4, width), bf16),
            V((tokens // 4, width), bf16),
            *[V((tokens // 2, ahead), bf16)] * 2,
            *[V((own, ahead), bf16)] * 2,
            dma((8,)),
            dma((3, WEIGHT_CHUNKS)),
            dma((2, n_sec)),
            dma((2, n_sec)),
            dma((n_sec,)),
            dma((n_sec,)),
            *[dma((3, GATHER_CHUNKS))] * 2,
            *[dma((n_sec, GATHER_CHUNKS))] * 4,
            *[dma((2, GATHER_CHUNKS))] * 2,
            *[dma((len(RETURN_EIGHTHS),))] * 4,
            *[dma((len(RETURN_EIGHTHS), n_sec))] * 2,
            *[dma((n_sec, 2))] * 2,
            *[dma((1,))] * 2,
        ],
        compiler_params=pltpu.CompilerParams(
            collective_id=0, has_side_effects=True, vmem_limit_bytes=66900000
        ),
    )(
        doc_lengths,
        query,
        keys,
        values,
        residual,
        out_weight,
        norm_gain.reshape(1, width),
        expert_ids.T,
        gate_codes.T,
        w_gate,
        w_up,
        w_down,
    )


def whole_in_vmem(mesh):
    shape = mesh.shape
    return shape["tp"] == 2 and shape["pp"] == 2 and shape["sec"] > 1 and E % shape["sec"] == 0


def solution(mesh):
    in_specs = (
        P(("groups", "sec"), ("tp", "pp")),
        P(("groups", "sec"), "tp"),
        P(("groups", "sec"), "tp"),
        P(("groups", "sec"), None),
        P(("tp", "pp"), None),
        P(),
        P(("groups", "sec"), None),
        P(("groups", "sec"), None),
        P("groups"),
        P(("tp", "pp"), None, "sec"),
        P(("tp", "pp"), None, "sec"),
        P(("tp", "pp"), "sec", None),
    )
    out_specs = P(("groups", "sec", "tp", "pp"), None)
    return jax.shard_map(
        fused_device if whole_in_vmem(mesh) else per_device,
        mesh=mesh,
        in_specs=in_specs,
        out_specs=out_specs,
        check_vma=False,
    )
```
